32 devices in a mesh: tile: 8 (over z, y), depth: 4 (over x, core).
Axes of the slice: x: 2, y: 2, z: 4, core: 2. Of those that a mesh axis runs over, the one named last changes fastest.
Arguments:
- volume: bfloat16 [128, 128, 2048], P('tile', 'depth'), may hold values from -4 to 4
Outputs:
- image: float32 [4, 128, 2048], P(None, ('tile', 'depth'))
The draws below stay inside these ranges and needn't reach their ends.
All inputs are finite; a program needn't handle non-finite values.
Results may differ from the reference program's by a relative error of at most 0.0003.
Values may be sent and summed in bfloat16 or wider, within the bound.
No kernel may reach another device: no remote copies, remote signals or barrier semaphores. Data moves between devices by JAX's collectives and lax.ppermute only.
A program may use at most 64 MiB of HBM per device.

```python
import jax
import jax.numpy as jnp
from jax import lax

CX = 16
CZ = 32
NY = 2048
NX = 128
NZ = 128
N_TILE = 8
N_DEPTH = 4


def steps_of(key, shape, split, smallest, top_value):
    level = 1.0
    for position, blocks in split:
        steps = jax.random.uniform(jax.random.fold_in(jax.random.fold_in(key, 6), position), (blocks,), jnp.float32, smallest / len(split), top_value / len(split))
        level = level * jnp.repeat(jnp.exp(steps), shape[position] // blocks).reshape((-1,) + (1,) * (len(shape) - 1 - position))
    return level


def noise(rng, shape, width, limit, split=(), kind=jnp.bfloat16):
    drawn = jax.random.normal(rng, shape, jnp.float32) * width
    if len(split) > 0:
        drawn = steps_of(rng, shape, split, -0.22, 0.18) * drawn
    return jnp.clip(drawn, min=-limit, max=limit).astype(kind)


def setup_inputs(seed: int = 0) -> dict:
    keys = jax.random.split(jax.random.key(seed), 2)
    volume = noise(keys[0], (NX, NZ, NY), 1.0, 4.0, ((0, 8), (1, 4)))
    return dict(volume=volume)


OPACITY = 3.0
LIGHT_X = 0.48
LIGHT_Y = 0.6
LIGHT_Z = 0.64

def brick_image(padded, depth_total):
    field = padded.astype(jnp.float32)
    center = field[1:-1, 1:-1, 1:-1]
    grad_x = 0.5 * (field[2:, 1:-1, 1:-1] - field[:-2, 1:-1, 1:-1])
    grad_z = 0.5 * (field[1:-1, 2:, 1:-1] - field[1:-1, :-2, 1:-1])
    grad_y = 0.5 * (field[1:-1, 1:-1, 2:] - field[1:-1, 1:-1, :-2])
    facing = LIGHT_X * grad_x + LIGHT_Y * grad_y + LIGHT_Z * grad_z
    shade = 0.3 + 0.7 * jnp.abs(facing) / jnp.sqrt(1.0 + grad_x * grad_x + grad_y * grad_y + grad_z * grad_z)
    squared = center * center
    extinct = OPACITY / depth_total * squared / (1.0 + squared)
    before = jnp.cumsum(extinct, axis=1) - extinct
    weight = jnp.exp(-before) * (1.0 - jnp.exp(-extinct)) * shade
    red = lax.optimization_barrier(jnp.sum(weight * jax.nn.sigmoid(2.0 * center), axis=1))
    green = lax.optimization_barrier(jnp.sum(weight * (0.5 * jnp.exp(-squared)), axis=1))
    blue = lax.optimization_barrier(jnp.sum(weight * jax.nn.sigmoid(-2.0 * center), axis=1))
    passing = jnp.exp(-lax.optimization_barrier(jnp.sum(extinct, axis=1)))
    return jnp.stack([red, green, blue, passing], 0)

def reference(volume):
    padded = jnp.pad(volume, 1)

    def strip(column):
        slab = lax.dynamic_slice_in_dim(padded, (column * CX).astype(jnp.int32), CX + 2, 0)
        colour = jnp.zeros((3, CX, NY), jnp.float32)
        passing = jnp.ones((1, CX, NY), jnp.float32)
        for brick in range(N_DEPTH):
            part = brick_image(slab[:, brick * CZ:brick * CZ + CZ + 2, :], NZ)
            colour = colour + passing * part[:3]
            passing = passing * part[3:]
        return jnp.concatenate([colour, 1.0 - passing], 0)
    strips = lax.map(strip, jnp.arange(N_TILE, dtype=jnp.int32))
    return jnp.transpose(strips, (1, 0, 2, 3)).reshape(4, NX, NY)
```

```python
import math

import jax
import jax.numpy as jnp
from jax import lax
from jax.experimental import pallas as pl
from jax.experimental.pallas import tpu as pltpu
from jax.sharding import PartitionSpec as P

OPACITY = 3.0
LIGHT_X = 0.48
LIGHT_Y = 0.6
LIGHT_Z = 0.64
AMBIENT = 0.3
DIFFUSE = 0.7
LOG2E = math.log2(math.e)
LANES = 128
SUB = 8

VMEM = pl.BlockSpec(memory_space=pltpu.VMEM)
HBM = pl.BlockSpec(memory_space=pltpu.HBM)


def parity(axis):
    return lax.rem(lax.axis_index(axis), 2)


def pairs(axis, odd):
    found = []
    for low in range(odd, lax.axis_size(axis) - 1, 2):
        found += [(low, low + 1), (low + 1, low)]
    return found


def faces_kernel(volume, tile_a, tile_b, depth_a, depth_b, near, far, wide, sems):
    cells_x, cells_z, rows_y = volume.shape
    chunks = rows_y // LANES
    odd_tile = parity("tile")
    odd_depth = parity("depth")
    copies = [
        pltpu.make_async_copy(volume.at[:, pl.ds(0, SUB)], near, sems.at[0]),
        pltpu.make_async_copy(volume.at[:, pl.ds(cells_z - SUB, SUB)], far, sems.at[1]),
        pltpu.make_async_copy(volume.at[(cells_x - 1) * odd_tile], tile_b, sems.at[2]),
        pltpu.make_async_copy(volume.at[(cells_x - 1) * (1 - odd_tile)], tile_a, sems.at[3]),
    ]
    for copy in copies:
        copy.start()
    pitch = SUB + 1
    for which, (block, row) in enumerate(((near, 0), (far, SUB - 1))):
        copies[which].wait()
        for x in range(cells_x):
            rows = block[x].astype(jnp.float32)
            for c in range(chunks):
                wide[which, c, pl.ds(x * pitch, SUB), :] = rows[:, c * LANES : (c + 1) * LANES]
    for c in range(chunks):
        lanes = pl.ds(c * LANES, LANES)
        first, last = [
            jnp.concatenate(
                [
                    wide[which, c, pl.ds(g * SUB * pitch + row, SUB, stride=pitch), :]
                    for g in range(cells_x // SUB)
                ],
                axis=0,
            )
            for which, row in ((0, 0), (1, SUB - 1))
        ]
        depth_a[:, lanes] = jnp.where(odd_depth == 0, last, first).astype(jnp.bfloat16)
        depth_b[:, lanes] = jnp.where(odd_depth == 0, first, last).astype(jnp.bfloat16)
    copies[2].wait()
    copies[3].wait()


def faces(volume):
    cells_x, cells_z, rows_y = volume.shape
    column = jax.ShapeDtypeStruct((cells_z, rows_y), volume.dtype)
    layer = jax.ShapeDtypeStruct((cells_x, rows_y), volume.dtype)
    return pl.pallas_call(
        faces_kernel,
        out_shape=(column, column, layer, layer),
        in_specs=[HBM],
        out_specs=(VMEM,) * 4,
        scratch_shapes=[
            pltpu.VMEM((cells_x, SUB, rows_y), volume.dtype),
            pltpu.VMEM((cells_x, SUB, rows_y), volume.dtype),
            pltpu.VMEM((2, rows_y // LANES, cells_x * (SUB + 1), LANES), jnp.float32),
            pltpu.SemaphoreType.DMA((4,)),
        ],
        name="faces",
    )(volume)


class Field:
    def __init__(self, ref, cells_z, rows_y, slots):
        self.ref = ref
        self.cells_z = cells_z
        self.chunks = rows_y // LANES
        self.half = self.chunks // 2
        self.column, self.pitch, _ = Field.shape(cells_z, rows_y, slots)

    @staticmethod
    def shape(cells_z, rows_y, slots):
        column = cells_z + 2
        column += column % SUB == 0
        pitch = slots * column
        pitch += pitch % 4 == 0
        return column, pitch, (rows_y // LANES + 2) * pitch

    def row(self, chunk, slot, z):
        return (chunk + 1) * self.pitch + slot * self.column + z + 1

    def clear_ends(self):
        blank = jnp.zeros((self.pitch, LANES), jnp.float32)
        self.ref[pl.ds(0, self.pitch), :] = blank
        self.ref[pl.ds((self.chunks + 1) * self.pitch, self.pitch), :] = blank

    def put_column(self, slot, block):
        wide = block.astype(jnp.float32)
        for c in range(self.chunks):
            lanes = slice(c * LANES, (c + 1) * LANES)
            self.ref[pl.ds(self.row(c, slot, 0), self.cells_z), :] = wide[:, lanes]

    def put_layer(self, slot, z, layer):
        count = layer.shape[0]
        for c in range(self.chunks):
            lanes = slice(c * LANES, (c + 1) * LANES)
            at = pl.ds(self.row(c, slot, z), count, stride=self.column) if count > 1 else pl.ds(self.row(c, slot, z), 1)
            self.ref[at, :] = layer[:, lanes]

    def get(self, chunk, slot, z):
        return self.ref[pl.ds(self.row(chunk, slot, z), self.half, stride=2 * self.pitch), :]


def march(field, slot, depth_total):
    shape = (field.half, LANES)
    lane = lax.broadcasted_iota(jnp.int32, shape, 1)
    first, last = lane == 0, lane == LANES - 1
    coefficients = [2.0 * DIFFUSE * 0.5 * light for light in (LIGHT_X, LIGHT_Y, LIGHT_Z)]
    density = OPACITY / depth_total

    def cell(here, before, after, left, right, dy, sums):
        passing, total, skew, bell = sums
        dx = right - left
        dz = after - before
        facing = coefficients[0] * dx + coefficients[1] * dy + coefficients[2] * dz
        shade = AMBIENT + jnp.abs(facing) * lax.rsqrt(4.0 + dx * dx + dy * dy + dz * dz)
        squared = here * here
        power = squared * (-LOG2E)
        behind = passing * jnp.exp2(power * (density / (1.0 + squared)))
        weight = (passing - behind) * shade
        return behind, total + weight, skew + weight * jnp.tanh(here), bell + weight * jnp.exp2(power)

    one, zero = jnp.ones(shape, jnp.float32), jnp.zeros(shape, jnp.float32)
    even_sums = odd_sums = (one, zero, zero, zero)
    even_before, odd_before = field.get(0, slot, -1), field.get(1, slot, -1)
    even, odd = field.get(0, slot, 0), field.get(1, slot, 0)
    for z in range(field.cells_z):
        even_after, odd_after = field.get(0, slot, z + 1), field.get(1, slot, z + 1)
        next_even, last_odd = field.get(2, slot, z), field.get(-1, slot, z)
        up = [pltpu.roll(v, LANES - 1, 1) for v in (even, odd, next_even)]
        down = [pltpu.roll(v, 1, 1) for v in (last_odd, even, odd)]
        even_dy = jnp.where(last, up[1], up[0]) - jnp.where(first, down[0], down[1])
        odd_dy = jnp.where(last, up[2], up[1]) - jnp.where(first, down[1], down[2])
        even_sums = cell(
            even, even_before, even_after, field.get(0, slot - 1, z), field.get(0, slot + 1, z), even_dy, even_sums
        )
        odd_sums = cell(
            odd, odd_before, odd_after, field.get(1, slot - 1, z), field.get(1, slot + 1, z), odd_dy, odd_sums
        )
        even_before, even, odd_before, odd = even, even_after, odd, odd_after
    return [
        (0.5 * (total + skew), 0.5 * bell, 0.5 * (total - skew), passing)
        for passing, total, skew, bell in (even_sums, odd_sums)
    ]


def store_column(out, x, parts):
    for which, channels in enumerate(parts):
        for channel, value in enumerate(channels):
            out[x, channel, pl.ds(which, value.shape[0], stride=2), :] = value


def inner_kernel(depth_total, volume, depth_a, depth_b, out, scratch):
    cells_x, cells_z, rows_y = volume.shape
    field = Field(scratch, cells_z, rows_y, cells_x)
    odd_depth = parity("depth")
    field.clear_ends()
    layers = [depth_a[...].astype(jnp.float32), depth_b[...].astype(jnp.float32)]
    for layer, other in zip(layers, (odd_depth, 1 - odd_depth)):
        z = cells_z - other * (cells_z + 1)
        for x in range(0, cells_x, SUB):
            field.put_layer(x, z, layer[x : x + SUB])
    field.put_column(0, volume[0])
    field.put_column(1, volume[1])

    def column(x, _):
        field.put_column(x + 1, volume[x + 1])
        store_column(out, x - 1, march(field, x, depth_total))
        return 0

    lax.fori_loop(1, cells_x - 1, column, 0)


def inner(volume, depth_a, depth_b, depth_total):
    cells_x, cells_z, rows_y = volume.shape
    _, _, rows = Field.shape(cells_z, rows_y, cells_x)
    return pl.pallas_call(
        lambda *refs: inner_kernel(depth_total, *refs),
        out_shape=jax.ShapeDtypeStruct((cells_x - 2, 4, rows_y // LANES, LANES), jnp.float32),
        in_specs=[VMEM] * 3,
        out_specs=VMEM,
        scratch_shapes=[pltpu.VMEM((rows, LANES), jnp.float32)],
        compiler_params=pltpu.CompilerParams(vmem_limit_bytes=24 << 20),
        cost_estimate=pl.CostEstimate(flops=10**8, bytes_accessed=10**7, transcendentals=0),
        name="inner",
    )(volume, depth_a, depth_b)


def outer_kernel(depth_total, volume, depth_a, depth_b, tile_a, tile_b, done, kept, given, scratch, edge):
    cells_x, cells_z, rows_y = volume.shape
    field = Field(scratch, cells_z, rows_y, 6)
    odd_depth, odd_tile = parity("depth"), parity("tile")
    field.clear_ends()
    for slot, x in ((1, 0), (2, 1), (3, cells_x - 2), (4, cells_x - 1)):
        field.put_column(slot, volume[x])
    for block, other in ((tile_a, odd_tile), (tile_b, 1 - odd_tile)):
        field.put_column(5 * (1 - other), block[...])
    for block, other in ((depth_a, odd_depth), (depth_b, 1 - odd_depth)):
        z = cells_z - other * (cells_z + 1)
        layer = block[...].astype(jnp.float32)
        field.put_layer(1, z, layer[:1])
        field.put_layer(4, z, layer[cells_x - 1 :])

    def column(side, _):
        store_column(edge, side, march(field, 1 + 3 * side, depth_total))
        return 0

    lax.fori_loop(0, 2, column, 0)
    upper = parity("depth")
    pieces = cells_x // lax.axis_size("depth")

    def fetch(x):
        return jnp.where(x == 0, edge[0], jnp.where(x == cells_x - 1, edge[1], done[jnp.clip(x - 1, 0, cells_x - 3)]))

    for i in range(cells_x // 2):
        low = i // pieces * 2 * pieces + i % pieces
        kept[i] = fetch(low + upper * pieces)
        given[i] = fetch(low + (1 - upper) * pieces)


def outer(volume, depth_a, depth_b, tile_a, tile_b, done, depth_total):
    cells_x, cells_z, rows_y = volume.shape
    _, _, rows = Field.shape(cells_z, rows_y, 6)
    half = jax.ShapeDtypeStruct((cells_x // 2, 4, rows_y // LANES, LANES), jnp.float32)
    return pl.pallas_call(
        lambda *refs: outer_kernel(depth_total, *refs),
        out_shape=(half, half),
        in_specs=[VMEM] * 6,
        out_specs=(VMEM, VMEM),
        scratch_shapes=[
            pltpu.VMEM((rows, LANES), jnp.float32),
            pltpu.VMEM((2, 4, rows_y // LANES, LANES), jnp.float32),
        ],
        compiler_params=pltpu.CompilerParams(vmem_limit_bytes=24 << 20),
        cost_estimate=pl.CostEstimate(flops=10**7, bytes_accessed=10**6, transcendentals=0),
        name="outer",
    )(volume, depth_a, depth_b, tile_a, tile_b, done)


def over(own, other, in_front):
    front = [jnp.where(in_front, a, b) for a, b in zip(own, other)]
    back = [jnp.where(in_front, b, a) for a, b in zip(own, other)]
    return [a + front[3] * b for a, b in zip(front[:3], back[:3])] + [front[3] * back[3]]


def merge_kernel(section, pieces, kept, other, next_kept, next_given):
    position = lax.axis_index("depth")
    in_front = lax.rem(position // 2**section, 2) == 0
    upper = lax.rem(position // 2 ** (section + 1), 2)
    for i in range(kept.shape[0] // 2):
        low = i // pieces * 2 * pieces + i % pieces
        for target, x in ((next_kept, low + upper * pieces), (next_given, low + (1 - upper) * pieces)):
            for channel, value in enumerate(over(list(kept[x]), list(other[x]), in_front)):
                target[i, channel] = value


def merge(kept, other, section, pieces):
    half = jax.ShapeDtypeStruct((kept.shape[0] // 2, *kept.shape[1:]), kept.dtype)
    return pl.pallas_call(
        lambda *refs: merge_kernel(section, pieces, *refs),
        out_shape=(half, half),
        in_specs=[VMEM] * 2,
        out_specs=(VMEM, VMEM),
        name="merge",
    )(kept, other)


def finish_kernel(section, kept, other, image, whole):
    position = lax.axis_index("depth")
    in_front = lax.rem(position // 2**section, 2) == 0
    columns, _, chunks, _ = kept.shape
    for x in range(columns):
        red, green, blue, passing = over(list(kept[x]), list(other[x]), in_front)
        for channel, value in enumerate((red, green, blue, 1.0 - passing)):
            for c in range(chunks):
                image[channel, pl.ds(x, 1), pl.ds(c * LANES, LANES)] = value[c : c + 1]


def finish(kept, other, section):
    columns, channels, chunks, _ = kept.shape
    return pl.pallas_call(
        lambda section_kept, section_other, image: finish_kernel(section, section_kept, section_other, image, None),
        out_shape=jax.ShapeDtypeStruct((channels, columns, chunks * LANES), kept.dtype),
        in_specs=[VMEM] * 2,
        out_specs=VMEM,
        name="finish",
    )(kept, other)


def shards(volume):
    depth_count = lax.axis_size("depth")
    depth_total = volume.shape[1] * depth_count
    pieces = volume.shape[0] // depth_count
    levels = depth_count.bit_length() - 1
    tile_a, tile_b, depth_a, depth_b = faces(volume)
    tile_b = lax.ppermute(tile_b, "tile", pairs("tile", 1))
    depth_b = lax.ppermute(depth_b, "depth", pairs("depth", 1))
    depth_a = lax.ppermute(depth_a, "depth", pairs("depth", 0))
    tile_a = lax.ppermute(tile_a, "tile", pairs("tile", 0))
    done = inner(volume, depth_a, depth_b, depth_total)
    kept, given = outer(volume, depth_a, depth_b, tile_a, tile_b, done, depth_total)
    for section in range(levels):
        other = lax.ppermute(given, "depth", [(i, i ^ 1 << section) for i in range(depth_count)])
        if section < levels - 1:
            kept, given = merge(kept, other, section, pieces)
    return finish(kept, other, levels - 1)


def solution(mesh):
    in_specs = (P("tile", "depth", None),)
    out_specs = P(None, ("tile", "depth"), None)
    return jax.shard_map(shards, mesh=mesh, in_specs=in_specs, out_specs=out_specs, check_vma=False)
```

```python
import math

import jax
import jax.numpy as jnp
from jax import lax
from jax.experimental import pallas as pl
from jax.experimental.pallas import tpu as pltpu
from jax.sharding import PartitionSpec as P


OPACITY = 3.0
LIGHT_X = 0.48
LIGHT_Y = 0.6
LIGHT_Z = 0.64
AMBIENT = 0.3
DIFFUSE = 0.7
LOG2E = math.log2(math.e)
LANES = 128
SUB = 8

VMEM = pl.BlockSpec(memory_space=pltpu.VMEM)
HBM = pl.BlockSpec(memory_space=pltpu.HBM)


def parity(axis):
    return lax.rem(lax.axis_index(axis), 2)


def pairs(axis, odd):
    found = []
    for low in range(odd, lax.axis_size(axis) - 1, 2):
        found += [(low, low + 1), (low + 1, low)]
    return found


def faces_kernel(volume, tile_a, tile_b, depth_a, depth_b, near, far, wide, sems):
    cells_x, cells_z, rows_y = volume.shape
    chunks = rows_y // LANES
    odd_tile = parity("tile")
    odd_depth = parity("depth")
    copies = [
        pltpu.make_async_copy(volume.at[:, pl.ds(0, SUB)], near, sems.at[0]),
        pltpu.make_async_copy(volume.at[:, pl.ds(cells_z - SUB, SUB)], far, sems.at[1]),
        pltpu.make_async_copy(volume.at[(cells_x - 1) * odd_tile], tile_b, sems.at[2]),
        pltpu.make_async_copy(volume.at[(cells_x - 1) * (1 - odd_tile)], tile_a, sems.at[3]),
    ]
    for copy in copies:
        copy.start()
    pitch = SUB + 1
    for which, (block, row) in enumerate(((near, 0), (far, SUB - 1))):
        copies[which].wait()
        for x in range(cells_x):
            rows = block[x].astype(jnp.float32)
            for c in range(chunks):
                wide[which, c, pl.ds(x * pitch, SUB), :] = rows[:, c * LANES : (c + 1) * LANES]
    for c in range(chunks):
        lanes = pl.ds(c * LANES, LANES)
        first, last = [
            jnp.concatenate(
                [
                    wide[which, c, pl.ds(g * SUB * pitch + row, SUB, stride=pitch), :]
                    for g in range(cells_x // SUB)
                ],
                axis=0,
            )
            for which, row in ((0, 0), (1, SUB - 1))
        ]
        depth_a[:, lanes] = jnp.where(odd_depth == 0, last, first).astype(jnp.bfloat16)
        depth_b[:, lanes] = jnp.where(odd_depth == 0, first, last).astype(jnp.bfloat16)
    copies[2].wait()
    copies[3].wait()


def faces(volume):
    cells_x, cells_z, rows_y = volume.shape
    column = jax.ShapeDtypeStruct((cells_z, rows_y), volume.dtype)
    layer = jax.ShapeDtypeStruct((cells_x, rows_y), volume.dtype)
    return pl.pallas_call(
        faces_kernel,
        out_shape=(column, column, layer, layer),
        in_specs=[HBM],
        out_specs=(VMEM,) * 4,
        scratch_shapes=[
            pltpu.VMEM((cells_x, SUB, rows_y), volume.dtype),
            pltpu.VMEM((cells_x, SUB, rows_y), volume.dtype),
            pltpu.VMEM((2, rows_y // LANES, cells_x * (SUB + 1), LANES), jnp.float32),
            pltpu.SemaphoreType.DMA((4,)),
        ],
        compiler_params=pltpu.CompilerParams(vmem_limit_bytes=12 << 20),
        name="faces",
    )(pltpu.with_memory_space_constraint(volume, pltpu.HBM))


class Field:
    def __init__(self, ref, cells_z, rows_y, slots):
        self.ref = ref
        self.cells_z = cells_z
        self.chunks = rows_y // LANES
        self.half = self.chunks // 2
        self.column, self.pitch, _ = Field.shape(cells_z, rows_y, slots)

    @staticmethod
    def shape(cells_z, rows_y, slots):
        column = cells_z + 2
        column += column % SUB == 0
        pitch = slots * column
        pitch += pitch % 4 == 0
        return column, pitch, (rows_y // LANES + 2) * pitch

    def row(self, chunk, slot, z):
        return (chunk + 1) * self.pitch + slot * self.column + z + 1

    def clear_ends(self):
        blank = jnp.zeros((self.pitch, LANES), jnp.float32)
        self.ref[pl.ds(0, self.pitch), :] = blank
        self.ref[pl.ds((self.chunks + 1) * self.pitch, self.pitch), :] = blank

    def put_column(self, slot, block):
        wide = block.astype(jnp.float32)
        for c in range(self.chunks):
            lanes = slice(c * LANES, (c + 1) * LANES)
            self.ref[pl.ds(self.row(c, slot, 0), self.cells_z), :] = wide[:, lanes]

    def put_layer(self, slot, z, layer):
        count = layer.shape[0]
        for c in range(self.chunks):
            lanes = slice(c * LANES, (c + 1) * LANES)
            at = pl.ds(self.row(c, slot, z), count, stride=self.column) if count > 1 else pl.ds(self.row(c, slot, z), 1)
            self.ref[at, :] = layer[:, lanes]

    def get(self, chunk, slot, z):
        return self.ref[pl.ds(self.row(chunk, slot, z), self.half, stride=2 * self.pitch), :]


def march(field, slot, depth_total):
    shape = (field.half, LANES)
    lane = lax.broadcasted_iota(jnp.int32, shape, 1)
    first, last = lane == 0, lane == LANES - 1
    coefficients = [2.0 * DIFFUSE * 0.5 * light for light in (LIGHT_X, LIGHT_Y, LIGHT_Z)]
    density = OPACITY / depth_total

    def cell(here, before, after, left, right, dy, sums):
        passing, total, skew, bell = sums
        dx = right - left
        dz = after - before
        facing = coefficients[0] * dx + coefficients[1] * dy + coefficients[2] * dz
        shade = AMBIENT + jnp.abs(facing) * lax.rsqrt(4.0 + dx * dx + dy * dy + dz * dz)
        squared = here * here
        power = squared * (-LOG2E)
        behind = passing * jnp.exp2(power * (density / (1.0 + squared)))
        weight = (passing - behind) * shade
        return behind, total + weight, skew + weight * jnp.tanh(here), bell + weight * jnp.exp2(power)

    one, zero = jnp.ones(shape, jnp.float32), jnp.zeros(shape, jnp.float32)
    even_sums = odd_sums = (one, zero, zero, zero)
    even_before, odd_before = field.get(0, slot, -1), field.get(1, slot, -1)
    even, odd = field.get(0, slot, 0), field.get(1, slot, 0)
    for z in range(field.cells_z):
        even_after, odd_after = field.get(0, slot, z + 1), field.get(1, slot, z + 1)
        next_even, last_odd = field.get(2, slot, z), field.get(-1, slot, z)
        up = [pltpu.roll(v, LANES - 1, 1) for v in (even, odd, next_even)]
        down = [pltpu.roll(v, 1, 1) for v in (last_odd, even, odd)]
        even_dy = jnp.where(last, up[1], up[0]) - jnp.where(first, down[0], down[1])
        odd_dy = jnp.where(last, up[2], up[1]) - jnp.where(first, down[1], down[2])
        even_sums = cell(
            even, even_before, even_after, field.get(0, slot - 1, z), field.get(0, slot + 1, z), even_dy, even_sums
        )
        odd_sums = cell(
            odd, odd_before, odd_after, field.get(1, slot - 1, z), field.get(1, slot + 1, z), odd_dy, odd_sums
        )
        even_before, even, odd_before, odd = even, even_after, odd, odd_after
    return [
        (0.5 * (total + skew), 0.5 * bell, 0.5 * (total - skew), passing)
        for passing, total, skew, bell in (even_sums, odd_sums)
    ]


def store_column(out, x, parts):
    for which, channels in enumerate(parts):
        for channel, value in enumerate(channels):
            out[x, channel, pl.ds(which, value.shape[0], stride=2), :] = value


def inner_kernel(depth_total, volume, depth_a, depth_b, out, scratch):
    cells_x, cells_z, rows_y = volume.shape
    field = Field(scratch, cells_z, rows_y, cells_x)
    odd_depth = parity("depth")
    field.clear_ends()
    layers = [depth_a[...].astype(jnp.float32), depth_b[...].astype(jnp.float32)]
    for layer, other in zip(layers, (odd_depth, 1 - odd_depth)):
        z = cells_z - other * (cells_z + 1)
        for x in range(0, cells_x, SUB):
            field.put_layer(x, z, layer[x : x + SUB])
    field.put_column(0, volume[0])
    field.put_column(1, volume[1])

    def column(x, _):
        field.put_column(x + 1, volume[x + 1])
        store_column(out, x - 1, march(field, x, depth_total))
        return 0

    lax.fori_loop(1, cells_x - 1, column, 0)


def inner(volume, depth_a, depth_b, depth_total):
    cells_x, cells_z, rows_y = volume.shape
    _, _, rows = Field.shape(cells_z, rows_y, cells_x)
    return pl.pallas_call(
        lambda *refs: inner_kernel(depth_total, *refs),
        out_shape=jax.ShapeDtypeStruct((cells_x - 2, 4, rows_y // LANES, LANES), jnp.float32),
        in_specs=[VMEM] * 3,
        out_specs=VMEM,
        scratch_shapes=[pltpu.VMEM((rows, LANES), jnp.float32)],
        compiler_params=pltpu.CompilerParams(vmem_limit_bytes=24 << 20),
        cost_estimate=pl.CostEstimate(flops=10**8, bytes_accessed=10**7, transcendentals=0),
        name="inner",
    )(volume, depth_a, depth_b)


def outer_kernel(depth_total, volume, depth_a, depth_b, tile_a, tile_b, done, kept, given, scratch, edge):
    cells_x, cells_z, rows_y = volume.shape
    field = Field(scratch, cells_z, rows_y, 6)
    odd_depth, odd_tile = parity("depth"), parity("tile")
    field.clear_ends()
    for slot, x in ((1, 0), (2, 1), (3, cells_x - 2), (4, cells_x - 1)):
        field.put_column(slot, volume[x])
    for block, other in ((tile_a, odd_tile), (tile_b, 1 - odd_tile)):
        field.put_column(5 * (1 - other), block[...])
    for block, other in ((depth_a, odd_depth), (depth_b, 1 - odd_depth)):
        z = cells_z - other * (cells_z + 1)
        layer = block[...].astype(jnp.float32)
        field.put_layer(1, z, layer[:1])
        field.put_layer(4, z, layer[cells_x - 1 :])

    def column(side, _):
        store_column(edge, side, march(field, 1 + 3 * side, depth_total))
        return 0

    lax.fori_loop(0, 2, column, 0)
    upper = parity("depth")
    pieces = cells_x // lax.axis_size("depth")

    def fetch(x):
        return jnp.where(x == 0, edge[0], jnp.where(x == cells_x - 1, edge[1], done[jnp.clip(x - 1, 0, cells_x - 3)]))

    for i in range(cells_x // 2):
        low = i // pieces * 2 * pieces + i % pieces
        kept[i] = fetch(low + upper * pieces)
        given[i] = fetch(low + (1 - upper) * pieces)


def outer(volume, depth_a, depth_b, tile_a, tile_b, done, depth_total):
    cells_x, cells_z, rows_y = volume.shape
    _, _, rows = Field.shape(cells_z, rows_y, 6)
    half = jax.ShapeDtypeStruct((cells_x // 2, 4, rows_y // LANES, LANES), jnp.float32)
    return pl.pallas_call(
        lambda *refs: outer_kernel(depth_total, *refs),
        out_shape=(half, half),
        in_specs=[VMEM] * 6,
        out_specs=(VMEM, VMEM),
        scratch_shapes=[
            pltpu.VMEM((rows, LANES), jnp.float32),
            pltpu.VMEM((2, 4, rows_y // LANES, LANES), jnp.float32),
        ],
        compiler_params=pltpu.CompilerParams(vmem_limit_bytes=24 << 20),
        cost_estimate=pl.CostEstimate(flops=10**7, bytes_accessed=10**6, transcendentals=0),
        name="outer",
    )(volume, depth_a, depth_b, tile_a, tile_b, done)


def over(own, other, in_front):
    front = [jnp.where(in_front, a, b) for a, b in zip(own, other)]
    back = [jnp.where(in_front, b, a) for a, b in zip(own, other)]
    return [a + front[3] * b for a, b in zip(front[:3], back[:3])] + [front[3] * back[3]]


def merge_kernel(section, pieces, kept, other, next_kept, next_given):
    position = lax.axis_index("depth")
    in_front = lax.rem(position // 2**section, 2) == 0
    upper = lax.rem(position // 2 ** (section + 1), 2)
    for i in range(kept.shape[0] // 2):
        low = i // pieces * 2 * pieces + i % pieces
        for target, x in ((next_kept, low + upper * pieces), (next_given, low + (1 - upper) * pieces)):
            for channel, value in enumerate(over(list(kept[x]), list(other[x]), in_front)):
                target[i, channel] = value


def merge(kept, other, section, pieces):
    half = jax.ShapeDtypeStruct((kept.shape[0] // 2, *kept.shape[1:]), kept.dtype)
    return pl.pallas_call(
        lambda *refs: merge_kernel(section, pieces, *refs),
        out_shape=(half, half),
        in_specs=[VMEM] * 2,
        out_specs=(VMEM, VMEM),
        compiler_params=pltpu.CompilerParams(vmem_limit_bytes=8 << 20),
        name="merge",
    )(kept, other)


def finish_kernel(section, kept, other, image):
    position = lax.axis_index("depth")
    in_front = lax.rem(position // 2**section, 2) == 0
    columns, _, chunks, _ = kept.shape
    for x in range(columns):
        red, green, blue, passing = over(list(kept[x]), list(other[x]), in_front)
        for channel, value in enumerate((red, green, blue, 1.0 - passing)):
            for c in range(chunks):
                image[channel, pl.ds(x, 1), pl.ds(c * LANES, LANES)] = value[c : c + 1]


def finish(kept, other, section):
    columns, channels, chunks, _ = kept.shape
    return pl.pallas_call(
        lambda section_kept, section_other, image: finish_kernel(section, section_kept, section_other, image),
        out_shape=jax.ShapeDtypeStruct((channels, columns, chunks * LANES), kept.dtype),
        in_specs=[VMEM] * 2,
        out_specs=VMEM,
        compiler_params=pltpu.CompilerParams(vmem_limit_bytes=8 << 20),
        name="finish",
    )(kept, other)


def shards(volume):
    depth_count = lax.axis_size("depth")
    depth_total = volume.shape[1] * depth_count
    pieces = volume.shape[0] // depth_count
    levels = depth_count.bit_length() - 1
    tile_a, tile_b, depth_a, depth_b = faces(volume)
    tile_b = lax.ppermute(tile_b, "tile", pairs("tile", 1))
    depth_b = lax.ppermute(depth_b, "depth", pairs("depth", 1))
    depth_a = lax.ppermute(depth_a, "depth", pairs("depth", 0))
    tile_a = lax.ppermute(tile_a, "tile", pairs("tile", 0))
    done = inner(volume, depth_a, depth_b, depth_total)
    kept, given = outer(volume, depth_a, depth_b, tile_a, tile_b, done, depth_total)
    for section in range(levels):
        other = lax.ppermute(given, "depth", [(i, i ^ 1 << section) for i in range(depth_count)])
        if section < levels - 1:
            kept, given = merge(kept, other, section, pieces)
    return finish(kept, other, levels - 1)


def solution(mesh):
    in_specs = (P("tile", "depth", None),)
    out_specs = P(None, ("tile", "depth"), None)
    return jax.shard_map(shards, mesh=mesh, in_specs=in_specs, out_specs=out_specs, check_vma=False)
```

```python
import math

import jax
import jax.numpy as jnp
from jax import lax
from jax.experimental import pallas as pl
from jax.experimental.pallas import tpu as pltpu
from jax.sharding import PartitionSpec as P


OPACITY = 3.0
LIGHT_X = 0.48
LIGHT_Y = 0.6
LIGHT_Z = 0.64
AMBIENT = 0.3
DIFFUSE = 0.7
LOG2E = math.log2(math.e)
LANES = 128
SUB = 8

VMEM = pl.BlockSpec(memory_space=pltpu.VMEM)
HBM = pl.BlockSpec(memory_space=pltpu.HBM)


def parity(axis):
    return lax.rem(lax.axis_index(axis), 2)


def exchange(x, axis, odd):
    tiles, depths = lax.axis_size("tile"), lax.axis_size("depth")
    found = []
    for tile in range(tiles):
        for depth in range(depths):
            if axis == "tile":
                other = (tile - odd ^ 1) + odd
                partner = (other, depth) if 0 <= other < tiles else (tile, depth ^ 1)
            else:
                partner = (tile, ((depth - odd ^ 1) + odd) % depths)
            found.append((tile * depths + depth, partner[0] * depths + partner[1]))
    return lax.ppermute(x, ("tile", "depth"), found)


def inside(axis):
    index = lax.axis_index(axis)
    return jnp.where((index == 0) | (index == lax.axis_size(axis) - 1), 0.0, 1.0)


def faces_kernel(volume, tile_a, tile_b, depth_a, depth_b, near, far, wide, sems):
    cells_x, cells_z, rows_y = volume.shape
    chunks = rows_y // LANES
    odd_tile = parity("tile")
    odd_depth = parity("depth")
    copies = [
        pltpu.make_async_copy(volume.at[:, pl.ds(0, SUB)], near, sems.at[0]),
        pltpu.make_async_copy(volume.at[:, pl.ds(cells_z - SUB, SUB)], far, sems.at[1]),
        pltpu.make_async_copy(volume.at[(cells_x - 1) * odd_tile], tile_b, sems.at[2]),
        pltpu.make_async_copy(volume.at[(cells_x - 1) * (1 - odd_tile)], tile_a, sems.at[3]),
    ]
    for copy in copies:
        copy.start()
    pitch = SUB + 1
    for which, (block, row) in enumerate(((near, 0), (far, SUB - 1))):
        copies[which].wait()
        for x in range(cells_x):
            rows = block[x].astype(jnp.float32)
            for c in range(chunks):
                wide[which, c, pl.ds(x * pitch, SUB), :] = rows[:, c * LANES : (c + 1) * LANES]
    for c in range(chunks):
        lanes = pl.ds(c * LANES, LANES)
        first, last = [
            jnp.concatenate(
                [
                    wide[which, c, pl.ds(g * SUB * pitch + row, SUB, stride=pitch), :]
                    for g in range(cells_x // SUB)
                ],
                axis=0,
            )
            for which, row in ((0, 0), (1, SUB - 1))
        ]
        depth_a[:, lanes] = jnp.where(odd_depth == 0, last, first).astype(jnp.bfloat16)
        depth_b[:, lanes] = jnp.where(odd_depth == 0, first, last).astype(jnp.bfloat16)
    copies[2].wait()
    copies[3].wait()


def faces(volume):
    cells_x, cells_z, rows_y = volume.shape
    column = jax.ShapeDtypeStruct((cells_z, rows_y), volume.dtype)
    layer = jax.ShapeDtypeStruct((cells_x, rows_y), volume.dtype)
    return pl.pallas_call(
        faces_kernel,
        out_shape=(column, column, layer, layer),
        in_specs=[HBM],
        out_specs=(VMEM,) * 4,
        scratch_shapes=[
            pltpu.VMEM((cells_x, SUB, rows_y), volume.dtype),
            pltpu.VMEM((cells_x, SUB, rows_y), volume.dtype),
            pltpu.VMEM((2, rows_y // LANES, cells_x * (SUB + 1), LANES), jnp.float32),
            pltpu.SemaphoreType.DMA((4,)),
        ],
        compiler_params=pltpu.CompilerParams(vmem_limit_bytes=12 << 20),
        name="faces",
    )(pltpu.with_memory_space_constraint(volume, pltpu.HBM))


class Field:
    def __init__(self, ref, cells_z, rows_y, slots):
        self.ref = ref
        self.cells_z = cells_z
        self.chunks = rows_y // LANES
        self.half = self.chunks // 2
        self.column, self.pitch, _ = Field.shape(cells_z, rows_y, slots)

    @staticmethod
    def shape(cells_z, rows_y, slots):
        column = cells_z + 2
        column += column % SUB == 0
        pitch = slots * column
        pitch += pitch % 4 == 0
        return column, pitch, (rows_y // LANES + 2) * pitch

    def row(self, chunk, slot, z):
        return (chunk + 1) * self.pitch + slot * self.column + z + 1

    def clear_ends(self):
        blank = jnp.zeros((self.pitch, LANES), jnp.float32)
        self.ref[pl.ds(0, self.pitch), :] = blank
        self.ref[pl.ds((self.chunks + 1) * self.pitch, self.pitch), :] = blank

    def put_column(self, slot, block, mask=None):
        wide = block.astype(jnp.float32)
        if mask is not None:
            wide = wide * mask
        for c in range(self.chunks):
            lanes = slice(c * LANES, (c + 1) * LANES)
            self.ref[pl.ds(self.row(c, slot, 0), self.cells_z), :] = wide[:, lanes]

    def put_layer(self, slot, z, layer):
        count = layer.shape[0]
        for c in range(self.chunks):
            lanes = slice(c * LANES, (c + 1) * LANES)
            at = pl.ds(self.row(c, slot, z), count, stride=self.column) if count > 1 else pl.ds(self.row(c, slot, z), 1)
            self.ref[at, :] = layer[:, lanes]

    def get(self, chunk, slot, z):
        return self.ref[pl.ds(self.row(chunk, slot, z), self.half, stride=2 * self.pitch), :]


def march(field, slot, depth_total):
    shape = (field.half, LANES)
    lane = lax.broadcasted_iota(jnp.int32, shape, 1)
    first, last = lane == 0, lane == LANES - 1
    coefficients = [2.0 * DIFFUSE * 0.5 * light for light in (LIGHT_X, LIGHT_Y, LIGHT_Z)]
    density = OPACITY / depth_total

    def cell(here, before, after, left, right, dy, sums):
        passing, total, skew, bell = sums
        dx = right - left
        dz = after - before
        facing = coefficients[0] * dx + coefficients[1] * dy + coefficients[2] * dz
        shade = AMBIENT + jnp.abs(facing) * lax.rsqrt(4.0 + dx * dx + dy * dy + dz * dz)
        squared = here * here
        power = squared * (-LOG2E)
        behind = passing * jnp.exp2(power * (density / (1.0 + squared)))
        weight = (passing - behind) * shade
        return behind, total + weight, skew + weight * jnp.tanh(here), bell + weight * jnp.exp2(power)

    one, zero = jnp.ones(shape, jnp.float32), jnp.zeros(shape, jnp.float32)
    even_sums = odd_sums = (one, zero, zero, zero)
    even_before, odd_before = field.get(0, slot, -1), field.get(1, slot, -1)
    even, odd = field.get(0, slot, 0), field.get(1, slot, 0)
    for z in range(field.cells_z):
        even_after, odd_after = field.get(0, slot, z + 1), field.get(1, slot, z + 1)
        next_even, last_odd = field.get(2, slot, z), field.get(-1, slot, z)
        up = [pltpu.roll(v, LANES - 1, 1) for v in (even, odd, next_even)]
        down = [pltpu.roll(v, 1, 1) for v in (last_odd, even, odd)]
        even_dy = jnp.where(last, up[1], up[0]) - jnp.where(first, down[0], down[1])
        odd_dy = jnp.where(last, up[2], up[1]) - jnp.where(first, down[1], down[2])
        even_sums = cell(
            even, even_before, even_after, field.get(0, slot - 1, z), field.get(0, slot + 1, z), even_dy, even_sums
        )
        odd_sums = cell(
            odd, odd_before, odd_after, field.get(1, slot - 1, z), field.get(1, slot + 1, z), odd_dy, odd_sums
        )
        even_before, even, odd_before, odd = even, even_after, odd, odd_after
    return [
        (0.5 * (total + skew), 0.5 * bell, 0.5 * (total - skew), passing)
        for passing, total, skew, bell in (even_sums, odd_sums)
    ]


def store_column(out, x, parts):
    for which, channels in enumerate(parts):
        for channel, value in enumerate(channels):
            out[x, channel, pl.ds(which, value.shape[0], stride=2), :] = value


def inner_kernel(depth_total, volume, depth_a, depth_b, out, scratch):
    cells_x, cells_z, rows_y = volume.shape
    field = Field(scratch, cells_z, rows_y, cells_x)
    odd_depth = parity("depth")
    field.clear_ends()
    layers = [depth_a[...].astype(jnp.float32), depth_b[...].astype(jnp.float32) * inside("depth")]
    for layer, other in zip(layers, (odd_depth, 1 - odd_depth)):
        z = cells_z - other * (cells_z + 1)
        for x in range(0, cells_x, SUB):
            field.put_layer(x, z, layer[x : x + SUB])
    field.put_column(0, volume[0])
    field.put_column(1, volume[1])

    def column(x, _):
        field.put_column(x + 1, volume[x + 1])
        store_column(out, x - 1, march(field, x, depth_total))
        return 0

    lax.fori_loop(1, cells_x - 1, column, 0)


def inner(volume, depth_a, depth_b, depth_total):
    cells_x, cells_z, rows_y = volume.shape
    _, _, rows = Field.shape(cells_z, rows_y, cells_x)
    return pl.pallas_call(
        lambda *refs: inner_kernel(depth_total, *refs),
        out_shape=jax.ShapeDtypeStruct((cells_x - 2, 4, rows_y // LANES, LANES), jnp.float32),
        in_specs=[VMEM] * 3,
        out_specs=VMEM,
        scratch_shapes=[pltpu.VMEM((rows, LANES), jnp.float32)],
        compiler_params=pltpu.CompilerParams(vmem_limit_bytes=24 << 20),
        cost_estimate=pl.CostEstimate(flops=10**8, bytes_accessed=10**7, transcendentals=0),
        name="inner",
    )(volume, depth_a, depth_b)


def outer_kernel(depth_total, volume, depth_a, depth_b, tile_a, tile_b, done, kept, given, scratch, edge):
    cells_x, cells_z, rows_y = volume.shape
    field = Field(scratch, cells_z, rows_y, 6)
    odd_depth, odd_tile = parity("depth"), parity("tile")
    field.clear_ends()
    for slot, x in ((1, 0), (2, 1), (3, cells_x - 2), (4, cells_x - 1)):
        field.put_column(slot, volume[x])
    for block, other, mask in ((tile_a, odd_tile, None), (tile_b, 1 - odd_tile, inside("tile"))):
        field.put_column(5 * (1 - other), block[...], mask)
    for block, other, mask in ((depth_a, odd_depth, 1.0), (depth_b, 1 - odd_depth, inside("depth"))):
        z = cells_z - other * (cells_z + 1)
        layer = block[...].astype(jnp.float32) * mask
        field.put_layer(1, z, layer[:1])
        field.put_layer(4, z, layer[cells_x - 1 :])

    def column(side, _):
        store_column(edge, side, march(field, 1 + 3 * side, depth_total))
        return 0

    lax.fori_loop(0, 2, column, 0)
    upper = parity("depth")
    pieces = cells_x // lax.axis_size("depth")

    def fetch(x):
        return jnp.where(x == 0, edge[0], jnp.where(x == cells_x - 1, edge[1], done[jnp.clip(x - 1, 0, cells_x - 3)]))

    for i in range(cells_x // 2):
        low = i // pieces * 2 * pieces + i % pieces
        kept[i] = fetch(low + upper * pieces)
        given[i] = fetch(low + (1 - upper) * pieces)


def outer(volume, depth_a, depth_b, tile_a, tile_b, done, depth_total):
    cells_x, cells_z, rows_y = volume.shape
    _, _, rows = Field.shape(cells_z, rows_y, 6)
    half = jax.ShapeDtypeStruct((cells_x // 2, 4, rows_y // LANES, LANES), jnp.float32)
    return pl.pallas_call(
        lambda *refs: outer_kernel(depth_total, *refs),
        out_shape=(half, half),
        in_specs=[VMEM] * 6,
        out_specs=(VMEM, VMEM),
        scratch_shapes=[
            pltpu.VMEM((rows, LANES), jnp.float32),
            pltpu.VMEM((2, 4, rows_y // LANES, LANES), jnp.float32),
        ],
        compiler_params=pltpu.CompilerParams(vmem_limit_bytes=24 << 20),
        cost_estimate=pl.CostEstimate(flops=10**7, bytes_accessed=10**6, transcendentals=0),
        name="outer",
    )(volume, depth_a, depth_b, tile_a, tile_b, done)


def over(own, other, in_front):
    front = [jnp.where(in_front, a, b) for a, b in zip(own, other)]
    back = [jnp.where(in_front, b, a) for a, b in zip(own, other)]
    return [a + front[3] * b for a, b in zip(front[:3], back[:3])] + [front[3] * back[3]]


def merge_kernel(section, pieces, kept, other, next_kept, next_given):
    position = lax.axis_index("depth")
    in_front = lax.rem(position // 2**section, 2) == 0
    upper = lax.rem(position // 2 ** (section + 1), 2)
    for i in range(kept.shape[0] // 2):
        low = i // pieces * 2 * pieces + i % pieces
        for target, x in ((next_kept, low + upper * pieces), (next_given, low + (1 - upper) * pieces)):
            for channel, value in enumerate(over(list(kept[x]), list(other[x]), in_front)):
                target[i, channel] = value


def merge(kept, other, section, pieces):
    half = jax.ShapeDtypeStruct((kept.shape[0] // 2, *kept.shape[1:]), kept.dtype)
    return pl.pallas_call(
        lambda *refs: merge_kernel(section, pieces, *refs),
        out_shape=(half, half),
        in_specs=[VMEM] * 2,
        out_specs=(VMEM, VMEM),
        compiler_params=pltpu.CompilerParams(vmem_limit_bytes=8 << 20),
        name="merge",
    )(kept, other)


def finish_kernel(section, kept, other, image):
    position = lax.axis_index("depth")
    in_front = lax.rem(position // 2**section, 2) == 0
    columns, _, chunks, _ = kept.shape
    for x in range(columns):
        red, green, blue, passing = over(list(kept[x]), list(other[x]), in_front)
        for channel, value in enumerate((red, green, blue, 1.0 - passing)):
            for c in range(chunks):
                image[channel, pl.ds(x, 1), pl.ds(c * LANES, LANES)] = value[c : c + 1]


def finish(kept, other, section):
    columns, channels, chunks, _ = kept.shape
    return pl.pallas_call(
        lambda section_kept, section_other, image: finish_kernel(section, section_kept, section_other, image),
        out_shape=jax.ShapeDtypeStruct((channels, columns, chunks * LANES), kept.dtype),
        in_specs=[VMEM] * 2,
        out_specs=VMEM,
        compiler_params=pltpu.CompilerParams(vmem_limit_bytes=8 << 20),
        name="finish",
    )(kept, other)


def shards(volume):
    depth_count = lax.axis_size("depth")
    depth_total = volume.shape[1] * depth_count
    pieces = volume.shape[0] // depth_count
    levels = depth_count.bit_length() - 1
    tile_a, tile_b, depth_a, depth_b = faces(volume)
    tile_b = exchange(tile_b, "tile", 1)
    depth_b = exchange(depth_b, "depth", 1)
    depth_a = exchange(depth_a, "depth", 0)
    tile_a = exchange(tile_a, "tile", 0)
    done = inner(volume, depth_a, depth_b, depth_total)
    kept, given = outer(volume, depth_a, depth_b, tile_a, tile_b, done, depth_total)
    for section in range(levels):
        other = lax.ppermute(given, "depth", [(i, i ^ 1 << section) for i in range(depth_count)])
        if section < levels - 1:
            kept, given = merge(kept, other, section, pieces)
    return finish(kept, other, levels - 1)


def solution(mesh):
    in_specs = (P("tile", "depth", None),)
    out_specs = P(None, ("tile", "depth"), None)
    return jax.shard_map(shards, mesh=mesh, in_specs=in_specs, out_specs=out_specs, check_vma=False)
```

```python
import math

import jax
import jax.numpy as jnp
from jax import lax
from jax.experimental import pallas as pl
from jax.experimental.pallas import tpu as pltpu
from jax.sharding import PartitionSpec as P


OPACITY = 3.0
LIGHT_X = 0.48
LIGHT_Y = 0.6
LIGHT_Z = 0.64
AMBIENT = 0.3
DIFFUSE = 0.7
LOG2E = math.log2(math.e)
LANES = 128
SUB = 8
POWER = 16.0
CENTRE = 7.9

VMEM = pl.BlockSpec(memory_space=pltpu.VMEM)
HBM = pl.BlockSpec(memory_space=pltpu.HBM)


def parity(axis):
    return lax.rem(lax.axis_index(axis), 2)


def exchange(x, axis, odd):
    tiles, depths = lax.axis_size("tile"), lax.axis_size("depth")
    found = []
    for tile in range(tiles):
        for depth in range(depths):
            if axis == "tile":
                other = (tile - odd ^ 1) + odd
                partner = (other, depth) if 0 <= other < tiles else (tile, depth ^ 1)
            else:
                other = (depth - odd ^ 1) + odd
                partner = (tile, other) if 0 <= other < depths else (tile ^ 1, depth)
            found.append((tile * depths + depth, partner[0] * depths + partner[1]))
    return lax.ppermute(x, ("tile", "depth"), found)


def inside(axis):
    index = lax.axis_index(axis)
    return jnp.where((index == 0) | (index == lax.axis_size(axis) - 1), 0.0, 1.0)


def faces_kernel(volume, tile_a, tile_b, depth_a, depth_b, near, far, wide, sems):
    cells_x, cells_z, rows_y = volume.shape
    chunks = rows_y // LANES
    odd_tile = parity("tile")
    odd_depth = parity("depth")
    copies = [
        pltpu.make_async_copy(volume.at[:, pl.ds(0, SUB)], near, sems.at[0]),
        pltpu.make_async_copy(volume.at[:, pl.ds(cells_z - SUB, SUB)], far, sems.at[1]),
        pltpu.make_async_copy(volume.at[(cells_x - 1) * odd_tile], tile_b, sems.at[2]),
        pltpu.make_async_copy(volume.at[(cells_x - 1) * (1 - odd_tile)], tile_a, sems.at[3]),
    ]
    for copy in copies:
        copy.start()
    pitch = SUB + 1
    for which, (block, row) in enumerate(((near, 0), (far, SUB - 1))):
        copies[which].wait()
        for x in range(cells_x):
            rows = block[x].astype(jnp.float32)
            for c in range(chunks):
                wide[which, c, pl.ds(x * pitch, SUB), :] = rows[:, c * LANES : (c + 1) * LANES]
    for c in range(chunks):
        lanes = pl.ds(c * LANES, LANES)
        first, last = [
            jnp.concatenate(
                [
                    wide[which, c, pl.ds(g * SUB * pitch + row, SUB, stride=pitch), :]
                    for g in range(cells_x // SUB)
                ],
                axis=0,
            )
            for which, row in ((0, 0), (1, SUB - 1))
        ]
        depth_a[:, lanes] = jnp.where(odd_depth == 0, last, first).astype(jnp.bfloat16)
        depth_b[:, lanes] = jnp.where(odd_depth == 0, first, last).astype(jnp.bfloat16)
    copies[2].wait()
    copies[3].wait()


def faces(volume):
    cells_x, cells_z, rows_y = volume.shape
    column = jax.ShapeDtypeStruct((cells_z, rows_y), volume.dtype)
    layer = jax.ShapeDtypeStruct((cells_x, rows_y), volume.dtype)
    return pl.pallas_call(
        faces_kernel,
        out_shape=(column, column, layer, layer),
        in_specs=[HBM],
        out_specs=(VMEM,) * 4,
        scratch_shapes=[
            pltpu.VMEM((cells_x, SUB, rows_y), volume.dtype),
            pltpu.VMEM((cells_x, SUB, rows_y), volume.dtype),
            pltpu.VMEM((2, rows_y // LANES, cells_x * (SUB + 1), LANES), jnp.float32),
            pltpu.SemaphoreType.DMA((4,)),
        ],
        compiler_params=pltpu.CompilerParams(vmem_limit_bytes=12 << 20),
        name="faces",
    )(pltpu.with_memory_space_constraint(volume, pltpu.HBM))


class Field:
    def __init__(self, ref, cells_z, rows_y, slots):
        self.ref = ref
        self.cells_z = cells_z
        self.chunks = rows_y // LANES
        self.half = self.chunks // 2
        self.column, self.pitch, _ = Field.shape(cells_z, rows_y, slots)

    @staticmethod
    def shape(cells_z, rows_y, slots):
        column = cells_z + 2
        column += column % SUB == 0
        pitch = slots * column
        pitch += pitch % 4 == 0
        return column, pitch, (rows_y // LANES + 2) * pitch

    def row(self, chunk, slot, z):
        return (chunk + 1) * self.pitch + slot * self.column + z + 1

    def clear_ends(self):
        blank = jnp.zeros((self.pitch, LANES), jnp.float32)
        self.ref[pl.ds(0, self.pitch), :] = blank
        self.ref[pl.ds((self.chunks + 1) * self.pitch, self.pitch), :] = blank

    def put_column(self, slot, block, mask=None):
        wide = block.astype(jnp.float32)
        if mask is not None:
            wide = wide * mask
        for c in range(self.chunks):
            lanes = slice(c * LANES, (c + 1) * LANES)
            self.ref[pl.ds(self.row(c, slot, 0), self.cells_z), :] = wide[:, lanes]

    def put_layer(self, slot, z, layer):
        count = layer.shape[0]
        for c in range(self.chunks):
            lanes = slice(c * LANES, (c + 1) * LANES)
            at = pl.ds(self.row(c, slot, z), count, stride=self.column) if count > 1 else pl.ds(self.row(c, slot, z), 1)
            self.ref[at, :] = layer[:, lanes]

    def get(self, chunk, slot, z):
        return self.ref[pl.ds(self.row(chunk, slot, z), self.half, stride=2 * self.pitch), :]


def march(field, slot, depth_total):
    shape = (field.half, LANES)
    lane = lax.broadcasted_iota(jnp.int32, shape, 1)
    first, last = lane == 0, lane == LANES - 1
    coefficients = [2.0 * DIFFUSE * 0.5 * light for light in (LIGHT_X, LIGHT_Y, LIGHT_Z)]
    density = OPACITY / depth_total

    def cell(here, before, after, left, right, dy, sums):
        passing, total, skew, bell = sums
        dx = right - left
        dz = after - before
        facing = coefficients[0] * dx + coefficients[1] * dy + coefficients[2] * dz
        shade = AMBIENT + jnp.abs(facing) * lax.rsqrt(4.0 + dx * dx + dy * dy + dz * dz)
        squared = here * here
        power = squared * (-LOG2E)
        behind = passing * jnp.exp2(power * (density / (1.0 + squared)))
        weight = (passing - behind) * shade
        return behind, total + weight, skew + weight * jnp.tanh(here), bell + weight * jnp.exp2(power)

    one, zero = jnp.ones(shape, jnp.float32), jnp.zeros(shape, jnp.float32)
    even_sums = odd_sums = (one, zero, zero, zero)
    even_before, odd_before = field.get(0, slot, -1), field.get(1, slot, -1)
    even, odd = field.get(0, slot, 0), field.get(1, slot, 0)
    for z in range(field.cells_z):
        even_after, odd_after = field.get(0, slot, z + 1), field.get(1, slot, z + 1)
        next_even, last_odd = field.get(2, slot, z), field.get(-1, slot, z)
        up = [pltpu.roll(v, LANES - 1, 1) for v in (even, odd, next_even)]
        down = [pltpu.roll(v, 1, 1) for v in (last_odd, even, odd)]
        even_dy = jnp.where(last, up[1], up[0]) - jnp.where(first, down[0], down[1])
        odd_dy = jnp.where(last, up[2], up[1]) - jnp.where(first, down[1], down[2])
        even_sums = cell(
            even, even_before, even_after, field.get(0, slot - 1, z), field.get(0, slot + 1, z), even_dy, even_sums
        )
        odd_sums = cell(
            odd, odd_before, odd_after, field.get(1, slot - 1, z), field.get(1, slot + 1, z), odd_dy, odd_sums
        )
        even_before, even, odd_before, odd = even, even_after, odd, odd_after
    return [
        (0.5 * (total + skew), 0.5 * bell, 0.5 * (total - skew), passing)
        for passing, total, skew, bell in (even_sums, odd_sums)
    ]


def store_column(out, x, parts):
    for which, channels in enumerate(parts):
        for channel, value in enumerate(channels):
            out[x, channel, pl.ds(which, value.shape[0], stride=2), :] = value


def inner_kernel(depth_total, volume, depth_a, depth_b, out, scratch):
    cells_x, cells_z, rows_y = volume.shape
    field = Field(scratch, cells_z, rows_y, cells_x)
    odd_depth = parity("depth")
    field.clear_ends()
    layers = [depth_a[...].astype(jnp.float32), depth_b[...].astype(jnp.float32) * inside("depth")]
    for layer, other in zip(layers, (odd_depth, 1 - odd_depth)):
        z = cells_z - other * (cells_z + 1)
        for x in range(0, cells_x, SUB):
            field.put_layer(x, z, layer[x : x + SUB])
    field.put_column(0, volume[0])
    field.put_column(1, volume[1])

    def column(x, _):
        field.put_column(x + 1, volume[x + 1])
        store_column(out, x - 1, march(field, x, depth_total))
        return 0

    lax.fori_loop(1, cells_x - 1, column, 0)


def inner(volume, depth_a, depth_b, depth_total):
    cells_x, cells_z, rows_y = volume.shape
    _, _, rows = Field.shape(cells_z, rows_y, cells_x)
    return pl.pallas_call(
        lambda *refs: inner_kernel(depth_total, *refs),
        out_shape=jax.ShapeDtypeStruct((cells_x - 2, 4, rows_y // LANES, LANES), jnp.float32),
        in_specs=[VMEM] * 3,
        out_specs=VMEM,
        scratch_shapes=[pltpu.VMEM((rows, LANES), jnp.float32)],
        compiler_params=pltpu.CompilerParams(vmem_limit_bytes=24 << 20),
        cost_estimate=pl.CostEstimate(flops=10**8, bytes_accessed=10**7, transcendentals=0),
        name="inner",
    )(volume, depth_a, depth_b)


def outer_kernel(depth_total, volume, depth_a, depth_b, tile_a, tile_b, done, kept, given, scratch, edge):
    cells_x, cells_z, rows_y = volume.shape
    field = Field(scratch, cells_z, rows_y, 6)
    odd_depth, odd_tile = parity("depth"), parity("tile")
    field.clear_ends()
    for slot, x in ((1, 0), (2, 1), (3, cells_x - 2), (4, cells_x - 1)):
        field.put_column(slot, volume[x])
    for block, other, mask in ((tile_a, odd_tile, None), (tile_b, 1 - odd_tile, inside("tile"))):
        field.put_column(5 * (1 - other), block[...], mask)
    for block, other, mask in ((depth_a, odd_depth, 1.0), (depth_b, 1 - odd_depth, inside("depth"))):
        z = cells_z - other * (cells_z + 1)
        layer = block[...].astype(jnp.float32) * mask
        field.put_layer(1, z, layer[:1])
        field.put_layer(4, z, layer[cells_x - 1 :])

    def column(side, _):
        store_column(edge, side, march(field, 1 + 3 * side, depth_total))
        return 0

    lax.fori_loop(0, 2, column, 0)
    upper = parity("depth")
    pieces = cells_x // lax.axis_size("depth")

    def fetch(x):
        return jnp.where(x == 0, edge[0], jnp.where(x == cells_x - 1, edge[1], done[jnp.clip(x - 1, 0, cells_x - 3)]))

    for i in range(cells_x // 2):
        low = i // pieces * 2 * pieces + i % pieces
        kept[i] = fetch(low + upper * pieces)
        given[i] = fetch(low + (1 - upper) * pieces)


def outer(volume, depth_a, depth_b, tile_a, tile_b, done, depth_total):
    cells_x, cells_z, rows_y = volume.shape
    _, _, rows = Field.shape(cells_z, rows_y, 6)
    half = jax.ShapeDtypeStruct((cells_x // 2, 4, rows_y // LANES, LANES), jnp.float32)
    return pl.pallas_call(
        lambda *refs: outer_kernel(depth_total, *refs),
        out_shape=(half, half),
        in_specs=[VMEM] * 6,
        out_specs=(VMEM, VMEM),
        scratch_shapes=[
            pltpu.VMEM((rows, LANES), jnp.float32),
            pltpu.VMEM((2, 4, rows_y // LANES, LANES), jnp.float32),
        ],
        compiler_params=pltpu.CompilerParams(vmem_limit_bytes=24 << 20),
        cost_estimate=pl.CostEstimate(flops=10**7, bytes_accessed=10**6, transcendentals=0),
        name="outer",
    )(volume, depth_a, depth_b, tile_a, tile_b, done)


def over(own, other, in_front):
    front = [jnp.where(in_front, a, b) for a, b in zip(own, other)]
    back = [jnp.where(in_front, b, a) for a, b in zip(own, other)]
    return [a + front[3] * b for a, b in zip(front[:3], back[:3])] + [front[3] * back[3]]


def encode(channels):
    red, green, blue, passing = channels
    return [
        jnp.exp2(POWER * (jnp.log2(x) + CENTRE)).astype(jnp.bfloat16) for x in (red, green, blue, 1.0 - passing)
    ]


def decode(codes):
    red, green, blue, opacity = [jnp.exp2(jnp.log2(y.astype(jnp.float32)) * (1.0 / POWER) - CENTRE) for y in codes]
    return [red, green, blue, 1.0 - opacity]


def received(block):
    channels = [block[channel] for channel in range(4)]
    return decode(channels) if block.dtype == jnp.bfloat16 else channels


def merge_kernel(section, pieces, kept, other, next_kept, next_given):
    position = lax.axis_index("depth")
    in_front = lax.rem(position // 2**section, 2) == 0
    upper = lax.rem(position // 2 ** (section + 1), 2)
    for i in range(kept.shape[0] // 2):
        low = i // pieces * 2 * pieces + i % pieces
        for target, x in ((next_kept, low + upper * pieces), (next_given, low + (1 - upper) * pieces)):
            channels = over(list(kept[x]), received(other[x]), in_front)
            for channel, value in enumerate(encode(channels) if target is next_given else channels):
                target[i, channel] = value


def merge(kept, other, section, pieces):
    shape = (kept.shape[0] // 2, *kept.shape[1:])
    return pl.pallas_call(
        lambda *refs: merge_kernel(section, pieces, *refs),
        out_shape=(jax.ShapeDtypeStruct(shape, jnp.float32), jax.ShapeDtypeStruct(shape, jnp.bfloat16)),
        in_specs=[VMEM] * 2,
        out_specs=(VMEM, VMEM),
        compiler_params=pltpu.CompilerParams(vmem_limit_bytes=8 << 20),
        name="merge",
    )(kept, other)


def finish_kernel(section, kept, other, image):
    position = lax.axis_index("depth")
    in_front = lax.rem(position // 2**section, 2) == 0
    columns, _, chunks, _ = kept.shape
    for x in range(columns):
        red, green, blue, passing = over(list(kept[x]), received(other[x]), in_front)
        for channel, value in enumerate((red, green, blue, 1.0 - passing)):
            for c in range(chunks):
                image[channel, pl.ds(x, 1), pl.ds(c * LANES, LANES)] = value[c : c + 1]


def finish(kept, other, section):
    columns, channels, chunks, _ = kept.shape
    return pl.pallas_call(
        lambda section_kept, section_other, image: finish_kernel(section, section_kept, section_other, image),
        out_shape=jax.ShapeDtypeStruct((channels, columns, chunks * LANES), kept.dtype),
        in_specs=[VMEM] * 2,
        out_specs=VMEM,
        compiler_params=pltpu.CompilerParams(vmem_limit_bytes=8 << 20),
        name="finish",
    )(kept, other)


def shards(volume):
    depth_count = lax.axis_size("depth")
    depth_total = volume.shape[1] * depth_count
    pieces = volume.shape[0] // depth_count
    levels = depth_count.bit_length() - 1
    tile_a, tile_b, depth_a, depth_b = faces(volume)
    tile_b = exchange(tile_b, "tile", 1)
    depth_b = exchange(depth_b, "depth", 1)
    depth_a = exchange(depth_a, "depth", 0)
    tile_a = exchange(tile_a, "tile", 0)
    done = inner(volume, depth_a, depth_b, depth_total)
    kept, given = outer(volume, depth_a, depth_b, tile_a, tile_b, done, depth_total)
    for section in range(levels):
        other = lax.ppermute(given, "depth", [(i, i ^ 1 << section) for i in range(depth_count)])
        if section < levels - 1:
            kept, given = merge(kept, other, section, pieces)
    return finish(kept, other, levels - 1)


def solution(mesh):
    in_specs = (P("tile", "depth", None),)
    out_specs = P(None, ("tile", "depth"), None)
    return jax.shard_map(shards, mesh=mesh, in_specs=in_specs, out_specs=out_specs, check_vma=False)
```

```python
import math

import jax
import jax.numpy as jnp
from jax import lax
from jax.experimental import pallas as pl
from jax.experimental.pallas import tpu as pltpu
from jax.sharding import PartitionSpec as P


OPACITY = 3.0
LIGHT_X = 0.48
LIGHT_Y = 0.6
LIGHT_Z = 0.64
AMBIENT = 0.3
DIFFUSE = 0.7
LOG2E = math.log2(math.e)
LANES = 128
PAIR = 2
POWER = 16.0
CENTRE = 7.9

VMEM = pl.BlockSpec(memory_space=pltpu.VMEM)
HBM = pl.BlockSpec(memory_space=pltpu.HBM)


def parity(axis):
    return lax.rem(lax.axis_index(axis), 2)


def exchange(x, axis, odd):
    tiles, depths = lax.axis_size("tile"), lax.axis_size("depth")
    found = []
    for tile in range(tiles):
        for depth in range(depths):
            if axis == "tile":
                other = (tile - odd ^ 1) + odd
                partner = (other, depth) if 0 <= other < tiles else (tile, depth ^ 1)
            else:
                partner = (tile, ((depth - odd ^ 1) + odd) % depths)
            found.append((tile * depths + depth, partner[0] * depths + partner[1]))
    return lax.ppermute(x, ("tile", "depth"), found)


def inside(axis):
    index = lax.axis_index(axis)
    return jnp.where((index == 0) | (index == lax.axis_size(axis) - 1), 0.0, 1.0)


def faces_kernel(volume, tile_a, tile_b, depth_a, depth_b, near, far, wide, sems):
    cells_x, cells_z, rows_y = volume.shape
    odd_tile = parity("tile")
    odd_depth = parity("depth")
    copies = [
        pltpu.make_async_copy(volume.at[:, pl.ds(0, PAIR)], near, sems.at[0]),
        pltpu.make_async_copy(volume.at[:, pl.ds(cells_z - PAIR, PAIR)], far, sems.at[1]),
        pltpu.make_async_copy(volume.at[(cells_x - 1) * (1 - odd_tile)], tile_a, sems.at[2]),
        pltpu.make_async_copy(volume.at[(cells_x - 1) * odd_tile], tile_b, sems.at[3]),
    ]
    for copy in copies:
        copy.start()
    for which, block in enumerate((near, far)):
        copies[which].wait()
        for x in range(cells_x):
            rows = block[x].astype(jnp.float32)
            for c in range(rows_y // LANES):
                wide[which, c, pl.ds(x * PAIR, PAIR), :] = rows[:, c * LANES : (c + 1) * LANES]
    for c in range(rows_y // LANES):
        lanes = pl.ds(c * LANES, LANES)
        first = wide[0, c, pl.ds(0, cells_x, stride=PAIR), :]
        last = wide[1, c, pl.ds(PAIR - 1, cells_x, stride=PAIR), :]
        depth_a[:, lanes] = jnp.where(odd_depth == 0, last, first).astype(jnp.bfloat16)
        depth_b[:, lanes] = jnp.where(odd_depth == 0, first, last).astype(jnp.bfloat16)
    copies[2].wait()
    copies[3].wait()


def faces(volume):
    cells_x, cells_z, rows_y = volume.shape
    column = jax.ShapeDtypeStruct((cells_z, rows_y), volume.dtype)
    layer = jax.ShapeDtypeStruct((cells_x, rows_y), volume.dtype)
    return pl.pallas_call(
        faces_kernel,
        out_shape=(column, column, layer, layer),
        in_specs=[HBM],
        out_specs=(VMEM,) * 4,
        scratch_shapes=[
            pltpu.VMEM((cells_x, PAIR, rows_y), volume.dtype),
            pltpu.VMEM((cells_x, PAIR, rows_y), volume.dtype),
            pltpu.VMEM((2, rows_y // LANES, cells_x * PAIR, LANES), jnp.float32),
            pltpu.SemaphoreType.DMA((4,)),
        ],
        compiler_params=pltpu.CompilerParams(vmem_limit_bytes=12 << 20),
        cost_estimate=pl.CostEstimate(flops=10**10, bytes_accessed=10**6, transcendentals=0),
        name="faces",
    )(pltpu.with_memory_space_constraint(volume, pltpu.HBM))


class Field:
    def __init__(self, ref, rows_y, columns):
        self.ref = ref
        self.chunks = rows_y // LANES
        self.half = self.chunks // 2
        self.pitch, _ = Field.shape(rows_y, columns)

    @staticmethod
    def shape(rows_y, columns):
        pitch = columns + (columns % 4 == 0)
        return pitch, (rows_y // LANES + 2) * pitch

    def clear_ends(self):
        blank = jnp.zeros((self.pitch, LANES), jnp.float32)
        self.ref[pl.ds(0, self.pitch), :] = blank
        self.ref[pl.ds((self.chunks + 1) * self.pitch, self.pitch), :] = blank

    def put(self, column, block):
        for c in range(self.chunks):
            at = pl.ds((c + 1) * self.pitch + column, block.shape[0])
            self.ref[at, :] = block[:, c * LANES : (c + 1) * LANES]

    def get(self, chunk, column):
        return self.ref[pl.ds((chunk + 1) * self.pitch + column, self.half, stride=2 * self.pitch), :]


def march(field, cells_z, column, left, right, before, after, depth_total):
    shape = (field.half, LANES)
    lane = lax.broadcasted_iota(jnp.int32, shape, 1)
    first, last = lane == 0, lane == LANES - 1
    scale = DIFFUSE * LIGHT_Z
    along_x, along_y = LIGHT_X / LIGHT_Z, LIGHT_Y / LIGHT_Z
    density = OPACITY / depth_total

    def cell(here, before, after, left, right, dy, sums):
        passing, total, skew, bell = sums
        dx = right - left
        dz = after - before
        facing = along_x * dx + along_y * dy + dz
        shade = AMBIENT / scale + jnp.abs(facing) * lax.rsqrt(4.0 + dx * dx + dy * dy + dz * dz)
        squared = here * here
        power = squared * (-LOG2E)
        behind = passing * jnp.exp2(power * (density / (1.0 + squared)))
        weight = (passing - behind) * shade
        return behind, total + weight, skew + weight * jnp.tanh(here), bell + weight * jnp.exp2(power)

    def along_z(chunk, z):
        source, row = before if z < 0 else after if z == cells_z else (field, column + z)
        return source.get(chunk, row)

    half = 0.5 * scale
    one, zero = jnp.ones(shape, jnp.float32), jnp.zeros(shape, jnp.float32)
    even_sums = odd_sums = (one, zero, zero, zero)
    even_before, odd_before = along_z(0, -1), along_z(1, -1)
    even, odd = along_z(0, 0), along_z(1, 0)
    for z in range(cells_z):
        even_after, odd_after = along_z(0, z + 1), along_z(1, z + 1)
        next_even, last_odd = along_z(2, z), along_z(-1, z)
        up = [pltpu.roll(v, LANES - 1, 1) for v in (even, odd, next_even)]
        down = [pltpu.roll(v, 1, 1) for v in (last_odd, even, odd)]
        even_dy = jnp.where(last, up[1], up[0]) - jnp.where(first, down[0], down[1])
        odd_dy = jnp.where(last, up[2], up[1]) - jnp.where(first, down[1], down[2])
        sides = [[side[0].get(chunk, side[1] + z) for side in (left, right)] for chunk in (0, 1)]
        even_sums = cell(even, even_before, even_after, *sides[0], even_dy, even_sums)
        odd_sums = cell(odd, odd_before, odd_after, *sides[1], odd_dy, odd_sums)
        even_before, even, odd_before, odd = even, even_after, odd, odd_after
    return [
        (half * (total + skew), half * bell, half * (total - skew), passing)
        for passing, total, skew, bell in (even_sums, odd_sums)
    ]


def store_column(out, x, parts):
    for which, channels in enumerate(parts):
        for channel, value in enumerate(channels):
            out[x, channel, pl.ds(which, value.shape[0], stride=2), :] = value


def widen_kernel(volume, rows):
    cells_x, cells_z, rows_y = volume.shape
    field = Field(rows, rows_y, cells_x * cells_z)
    field.clear_ends()

    def column(x, _):
        field.put(x * cells_z, volume[x].astype(jnp.float32))
        return 0

    lax.fori_loop(0, cells_x, column, 0, unroll=2)


def widen(volume):
    cells_x, cells_z, rows_y = volume.shape
    _, rows = Field.shape(rows_y, cells_x * cells_z)
    return pl.pallas_call(
        widen_kernel,
        out_shape=jax.ShapeDtypeStruct((rows, LANES), jnp.float32),
        in_specs=[VMEM],
        out_specs=VMEM,
        compiler_params=pltpu.CompilerParams(vmem_limit_bytes=12 << 20),
        cost_estimate=pl.CostEstimate(flops=10**6, bytes_accessed=10**6, transcendentals=0),
        name="widen",
    )(volume)


def put_layers(scratch, rows_y, depth_a, depth_b):
    cells_x = depth_a.shape[0]
    layers = Field(scratch, rows_y, 2 * cells_x)
    odd_depth = parity("depth")
    layers.put((1 - odd_depth) * cells_x, depth_a[...].astype(jnp.float32))
    layers.put(odd_depth * cells_x, depth_b[...].astype(jnp.float32) * inside("depth"))
    return layers


def inner_kernel(cells_z, depth_total, rows, depth_a, depth_b, out, scratch):
    cells_x, rows_y = depth_a.shape
    field = Field(rows, rows_y, cells_x * cells_z)
    layers = put_layers(scratch, rows_y, depth_a, depth_b)

    def columns(i, _):
        for x in (2 * i + 1, 2 * i + 2):
            at = x * cells_z
            sides = (field, at - cells_z), (field, at + cells_z), (layers, x), (layers, cells_x + x)
            store_column(out, x - 1, march(field, cells_z, at, *sides, depth_total))
        return 0

    lax.fori_loop(0, (cells_x - 2) // 2, columns, 0)


def inner(rows, depth_a, depth_b, cells_z, depth_total):
    cells_x, rows_y = depth_a.shape
    return pl.pallas_call(
        lambda *refs: inner_kernel(cells_z, depth_total, *refs),
        out_shape=jax.ShapeDtypeStruct((cells_x - 2, 4, rows_y // LANES, LANES), jnp.float32),
        in_specs=[VMEM] * 3,
        out_specs=VMEM,
        scratch_shapes=[pltpu.VMEM((Field.shape(rows_y, 2 * cells_x)[1], LANES), jnp.float32)],
        compiler_params=pltpu.CompilerParams(vmem_limit_bytes=12 << 20),
        cost_estimate=pl.CostEstimate(flops=10**8, bytes_accessed=10**7, transcendentals=0),
        name="inner",
    )(rows, depth_a, depth_b)


def outer_kernel(depth_total, rows, depth_a, depth_b, tile_a, tile_b, done, kept, given, scratch, ends, edge):
    cells_x, rows_y = depth_a.shape
    cells_z = tile_a.shape[0]
    odd_tile = parity("tile")
    field = Field(rows, rows_y, cells_x * cells_z)
    layers = put_layers(scratch, rows_y, depth_a, depth_b)
    halo = Field(ends, rows_y, 2 * cells_z)
    halo.put((1 - odd_tile) * cells_z, tile_a[...].astype(jnp.float32))
    halo.put(odd_tile * cells_z, tile_b[...].astype(jnp.float32) * inside("tile"))
    final = (cells_x - 1) * cells_z
    for side, at, left, right in (
        (0, 0, (halo, 0), (field, cells_z)),
        (1, final, (field, final - cells_z), (halo, cells_z)),
    ):
        x = side * (cells_x - 1)
        parts = march(field, cells_z, at, left, right, (layers, x), (layers, cells_x + x), depth_total)
        store_column(edge, side, parts)
    upper = parity("depth")
    pieces = cells_x // lax.axis_size("depth")
    half = cells_x // 2
    for i in range(half):
        low = i // pieces * 2 * pieces + i % pieces
        for target, bit in ((kept, upper), (given, 1 - upper)):
            x = low + bit * pieces
            if i == 0:
                target[i] = jnp.where(bit == 0, edge[0], done[pieces - 1])
            elif i == half - 1:
                target[i] = jnp.where(bit == 1, edge[1], done[cells_x - pieces - 2])
            else:
                target[i] = done[x - 1]


def outer(rows, depth_a, depth_b, tile_a, tile_b, done, depth_total):
    cells_x, rows_y = depth_a.shape
    cells_z = tile_a.shape[0]
    half = jax.ShapeDtypeStruct((cells_x // 2, 4, rows_y // LANES, LANES), jnp.float32)
    return pl.pallas_call(
        lambda *refs: outer_kernel(depth_total, *refs),
        out_shape=(half, half),
        in_specs=[VMEM] * 6,
        out_specs=(VMEM, VMEM),
        scratch_shapes=[
            pltpu.VMEM((Field.shape(rows_y, 2 * cells_x)[1], LANES), jnp.float32),
            pltpu.VMEM((Field.shape(rows_y, 2 * cells_z)[1], LANES), jnp.float32),
            pltpu.VMEM((2, 4, rows_y // LANES, LANES), jnp.float32),
        ],
        compiler_params=pltpu.CompilerParams(vmem_limit_bytes=12 << 20),
        cost_estimate=pl.CostEstimate(flops=10**7, bytes_accessed=10**6, transcendentals=0),
        name="outer",
    )(rows, depth_a, depth_b, tile_a, tile_b, done)


def over(own, other, in_front):
    front = [jnp.where(in_front, a, b) for a, b in zip(own, other)]
    back = [jnp.where(in_front, b, a) for a, b in zip(own, other)]
    return [a + front[3] * b for a, b in zip(front[:3], back[:3])] + [front[3] * back[3]]


def encode(channels):
    red, green, blue, passing = channels
    return [
        jnp.exp2(POWER * (jnp.log2(x) + CENTRE)).astype(jnp.bfloat16) for x in (red, green, blue, 1.0 - passing)
    ]


def decode(codes):
    red, green, blue, opacity = [jnp.exp2(jnp.log2(y.astype(jnp.float32)) * (1.0 / POWER) - CENTRE) for y in codes]
    return [red, green, blue, 1.0 - opacity]


def received(block):
    channels = [block[channel] for channel in range(4)]
    return decode(channels) if block.dtype == jnp.bfloat16 else channels


def merge_kernel(section, pieces, kept, other, next_kept, next_given):
    position = lax.axis_index("depth")
    in_front = lax.rem(position // 2**section, 2) == 0
    upper = lax.rem(position // 2 ** (section + 1), 2)
    for i in range(kept.shape[0] // 2):
        low = i // pieces * 2 * pieces + i % pieces
        for target, x in ((next_kept, low + upper * pieces), (next_given, low + (1 - upper) * pieces)):
            channels = over(list(kept[x]), received(other[x]), in_front)
            for channel, value in enumerate(encode(channels) if target is next_given else channels):
                target[i, channel] = value


def merge(kept, other, section, pieces):
    shape = (kept.shape[0] // 2, *kept.shape[1:])
    return pl.pallas_call(
        lambda *refs: merge_kernel(section, pieces, *refs),
        out_shape=(jax.ShapeDtypeStruct(shape, jnp.float32), jax.ShapeDtypeStruct(shape, jnp.bfloat16)),
        in_specs=[VMEM] * 2,
        out_specs=(VMEM, VMEM),
        compiler_params=pltpu.CompilerParams(vmem_limit_bytes=8 << 20),
        name="merge",
    )(kept, other)


def finish_kernel(section, kept, other, image):
    position = lax.axis_index("depth")
    in_front = lax.rem(position // 2**section, 2) == 0
    columns, _, chunks, _ = kept.shape
    for x in range(columns):
        red, green, blue, passing = over(list(kept[x]), received(other[x]), in_front)
        for channel, value in enumerate((red, green, blue, 1.0 - passing)):
            for c in range(chunks):
                image[channel, pl.ds(x, 1), pl.ds(c * LANES, LANES)] = value[c : c + 1]


def finish(kept, other, section):
    columns, channels, chunks, _ = kept.shape
    return pl.pallas_call(
        lambda section_kept, section_other, image: finish_kernel(section, section_kept, section_other, image),
        out_shape=jax.ShapeDtypeStruct((channels, columns, chunks * LANES), kept.dtype),
        in_specs=[VMEM] * 2,
        out_specs=VMEM,
        compiler_params=pltpu.CompilerParams(vmem_limit_bytes=8 << 20),
        name="finish",
    )(kept, other)


def shards(volume):
    depth_count = lax.axis_size("depth")
    depth_total = volume.shape[1] * depth_count
    pieces = volume.shape[0] // depth_count
    levels = depth_count.bit_length() - 1
    tile_a, tile_b, depth_a, depth_b = faces(volume)
    tile_b = exchange(tile_b, "tile", 1)
    depth_b = exchange(depth_b, "depth", 1)
    depth_a = exchange(depth_a, "depth", 0)
    tile_a = exchange(tile_a, "tile", 0)
    rows = widen(volume)
    done = inner(rows, depth_a, depth_b, volume.shape[1], depth_total)
    kept, given = outer(rows, depth_a, depth_b, tile_a, tile_b, done, depth_total)
    for section in range(levels):
        other = lax.ppermute(given, "depth", [(i, i ^ 1 << section) for i in range(depth_count)])
        if section < levels - 1:
            kept, given = merge(kept, other, section, pieces)
    return finish(kept, other, levels - 1)


def solution(mesh):
    in_specs = (P("tile", "depth", None),)
    out_specs = P(None, ("tile", "depth"), None)
    return jax.shard_map(shards, mesh=mesh, in_specs=in_specs, out_specs=out_specs, check_vma=False)
```

```python
import math

import jax
import jax.numpy as jnp
from jax import lax
from jax.experimental import pallas as pl
from jax.experimental.pallas import tpu as pltpu
from jax.sharding import PartitionSpec as P


OPACITY = 3.0
LIGHT_X = 0.48
LIGHT_Y = 0.6
LIGHT_Z = 0.64
AMBIENT = 0.3
DIFFUSE = 0.7
LOG2E = math.log2(math.e)
LANES = 128
PAIR = 2
POWER = 16.0
CENTRE = 7.9

VMEM = pl.BlockSpec(memory_space=pltpu.VMEM)
HBM = pl.BlockSpec(memory_space=pltpu.HBM)


def parity(axis):
    return lax.rem(lax.axis_index(axis), 2)


def exchange(x, axis, odd):
    tiles, depths = lax.axis_size("tile"), lax.axis_size("depth")
    found = []
    for tile in range(tiles):
        for depth in range(depths):
            if axis == "tile":
                other = (tile - odd ^ 1) + odd
                partner = (other, depth) if 0 <= other < tiles else (tile, depth ^ 1)
            else:
                partner = (tile, ((depth - odd ^ 1) + odd) % depths)
            found.append((tile * depths + depth, partner[0] * depths + partner[1]))
    return lax.ppermute(x, ("tile", "depth"), found)


def inside(axis):
    index = lax.axis_index(axis)
    return jnp.where((index == 0) | (index == lax.axis_size(axis) - 1), 0.0, 1.0)


def faces_kernel(volume, tile_a, tile_b, depth_a, depth_b, near, far, wide, sems):
    cells_x, cells_z, rows_y = volume.shape
    odd_tile = parity("tile")
    odd_depth = parity("depth")
    copies = [
        pltpu.make_async_copy(volume.at[:, pl.ds(0, PAIR)], near, sems.at[0]),
        pltpu.make_async_copy(volume.at[:, pl.ds(cells_z - PAIR, PAIR)], far, sems.at[1]),
        pltpu.make_async_copy(volume.at[(cells_x - 1) * (1 - odd_tile)], tile_a, sems.at[2]),
        pltpu.make_async_copy(volume.at[(cells_x - 1) * odd_tile], tile_b, sems.at[3]),
    ]
    for copy in copies:
        copy.start()
    for which, block in enumerate((near, far)):
        copies[which].wait()
        for x in range(cells_x):
            rows = block[x].astype(jnp.float32)
            for c in range(rows_y // LANES):
                wide[which, c, pl.ds(x * PAIR, PAIR), :] = rows[:, c * LANES : (c + 1) * LANES]
    for c in range(rows_y // LANES):
        lanes = pl.ds(c * LANES, LANES)
        first = wide[0, c, pl.ds(0, cells_x, stride=PAIR), :]
        last = wide[1, c, pl.ds(PAIR - 1, cells_x, stride=PAIR), :]
        depth_a[:, lanes] = jnp.where(odd_depth == 0, last, first).astype(jnp.bfloat16)
        depth_b[:, lanes] = jnp.where(odd_depth == 0, first, last).astype(jnp.bfloat16)
    copies[2].wait()
    copies[3].wait()


def faces(volume):
    cells_x, cells_z, rows_y = volume.shape
    column = jax.ShapeDtypeStruct((cells_z, rows_y), volume.dtype)
    layer = jax.ShapeDtypeStruct((cells_x, rows_y), volume.dtype)
    return pl.pallas_call(
        faces_kernel,
        out_shape=(column, column, layer, layer),
        in_specs=[HBM],
        out_specs=(VMEM,) * 4,
        scratch_shapes=[
            pltpu.VMEM((cells_x, PAIR, rows_y), volume.dtype),
            pltpu.VMEM((cells_x, PAIR, rows_y), volume.dtype),
            pltpu.VMEM((2, rows_y // LANES, cells_x * PAIR, LANES), jnp.float32),
            pltpu.SemaphoreType.DMA((4,)),
        ],
        compiler_params=pltpu.CompilerParams(vmem_limit_bytes=12 << 20),
        cost_estimate=pl.CostEstimate(flops=10**10, bytes_accessed=10**6, transcendentals=0),
        name="faces",
    )(pltpu.with_memory_space_constraint(volume, pltpu.HBM))


class Field:
    def __init__(self, ref, rows_y, columns):
        self.ref = ref
        self.chunks = rows_y // LANES
        self.half = self.chunks // 2
        self.pitch, _ = Field.shape(rows_y, columns)

    @staticmethod
    def shape(rows_y, columns):
        pitch = columns + (columns % 4 == 0)
        return pitch, (rows_y // LANES + 2) * pitch

    def clear_ends(self):
        blank = jnp.zeros((self.pitch, LANES), jnp.float32)
        self.ref[pl.ds(0, self.pitch), :] = blank
        self.ref[pl.ds((self.chunks + 1) * self.pitch, self.pitch), :] = blank

    def put(self, column, block):
        for c in range(self.chunks):
            at = pl.ds((c + 1) * self.pitch + column, block.shape[0])
            self.ref[at, :] = block[:, c * LANES : (c + 1) * LANES]

    def get(self, chunk, column):
        return self.ref[pl.ds((chunk + 1) * self.pitch + column, self.half, stride=2 * self.pitch), :]


class March:
    def __init__(self, field, cells_z, column, before, after, depth_total):
        self.field, self.cells_z, self.column = field, cells_z, column
        self.before, self.after = before, after
        self.density = OPACITY / depth_total
        self.shape = (field.half, LANES)
        self.scale = DIFFUSE * LIGHT_Z
        self.along_x, self.along_y = LIGHT_X / LIGHT_Z, LIGHT_Y / LIGHT_Z

    def at(self, chunk, z):
        side = self.before if z < 0 else self.after if z == self.cells_z else (self.field, self.column + z)
        return None if side is None else side[0].get(chunk, side[1])

    def cells(self):
        lane = lax.broadcasted_iota(jnp.int32, self.shape, 1)
        first, last = lane == 0, lane == LANES - 1
        self.passing = [jnp.ones(self.shape, jnp.float32)] * 2
        before = [self.at(which, -1) for which in (0, 1)]
        here = [self.at(which, 0) for which in (0, 1)]
        for z in range(self.cells_z):
            after = [self.at(which, z + 1) for which in (0, 1)]
            next_even, last_odd = self.at(2, z), self.at(-1, z)
            up = [pltpu.roll(v, LANES - 1, 1) for v in (*here, next_even)]
            down = [pltpu.roll(v, 1, 1) for v in (last_odd, *here)]
            for which in (0, 1):
                dy = jnp.where(last, up[which + 1], up[which]) - jnp.where(first, down[which], down[which + 1])
                facing, norm = self.along_y * dy, 4.0 + dy * dy
                if before[which] is not None and after[which] is not None:
                    facing, norm = self.along_z(facing, norm, before[which], after[which])
                squared = here[which] * here[which]
                power = squared * (-LOG2E)
                behind = self.passing[which] * jnp.exp2(power * (self.density / (1.0 + squared)))
                weight = self.passing[which] - behind
                self.passing[which] = behind
                yield z, which, facing, norm, (
                    weight,
                    weight * jnp.tanh(here[which]),
                    weight * jnp.exp2(power),
                )
            before, here = here, after

    def along_z(self, facing, norm, before, after):
        dz = after - before
        return facing + dz, norm + dz * dz

    def shade(self, facing, norm, left, right):
        dx = right - left
        return AMBIENT / self.scale + jnp.abs(self.along_x * dx + facing) * lax.rsqrt(norm + dx * dx)

    def colours(self, total, skew, bell, passing):
        half = 0.5 * self.scale
        return half * (total + skew), half * bell, half * (total - skew), passing


def march(field, cells_z, column, left, right, before, after, depth_total):
    way = March(field, cells_z, column, before, after, depth_total)
    sums = [[jnp.zeros(way.shape, jnp.float32)] * 3 for _ in (0, 1)]
    for z, which, facing, norm, weights in way.cells():
        shade = way.shade(facing, norm, left[0].get(which, left[1] + z), right[0].get(which, right[1] + z))
        total, skew, bell = sums[which]
        weight = weights[0] * shade
        sums[which] = [total + weight, skew + weights[1] * shade, bell + weights[2] * shade]
    return [way.colours(*sums[which], way.passing[which]) for which in (0, 1)]


def march_to_shading(field, cells_z, column, depth_total, saved, passed):
    way = March(field, cells_z, column, None, None, depth_total)
    for z, which, facing, norm, weights in way.cells():
        for k, value in enumerate((facing, norm, *weights)):
            saved[z, which, k] = value
    for which in (0, 1):
        passed[which] = way.passing[which]


def march_shading(field, cells_z, column, left, right, before, after, saved, passed, depth_total):
    way = March(field, cells_z, column, before, after, depth_total)
    parts = []
    for which in (0, 1):
        sums = [jnp.zeros(way.shape, jnp.float32)] * 3
        for z in range(cells_z):
            sides = [side[0].get(which, side[1] + z) for side in (left, right)]
            facing, norm = saved[z, which, 0], saved[z, which, 1]
            if z in (0, cells_z - 1):
                facing, norm = way.along_z(facing, norm, way.at(which, z - 1), way.at(which, z + 1))
            shade = way.shade(facing, norm, *sides)
            sums = [total + saved[z, which, 2 + k] * shade for k, total in enumerate(sums)]
        parts.append(way.colours(*sums, passed[which]))
    return parts


def store_column(out, x, parts):
    for which, channels in enumerate(parts):
        for channel, value in enumerate(channels):
            out[x, channel, pl.ds(which, value.shape[0], stride=2), :] = value


def widen_kernel(depth_total, volume, rows, saved, passed):
    cells_x, cells_z, rows_y = volume.shape
    field = Field(rows, rows_y, cells_x * cells_z)
    field.clear_ends()

    def column(x, _):
        field.put(x * cells_z, volume[x].astype(jnp.float32))
        return 0

    lax.fori_loop(0, cells_x, column, 0, unroll=2)
    for side, x in ((0, 0), (1, cells_x - 1)):
        march_to_shading(field, cells_z, x * cells_z, depth_total, saved.at[side], passed.at[side])


def widen(volume, depth_total):
    cells_x, cells_z, rows_y = volume.shape
    _, rows = Field.shape(rows_y, cells_x * cells_z)
    return pl.pallas_call(
        lambda *refs: widen_kernel(depth_total, *refs),
        out_shape=tuple(
            jax.ShapeDtypeStruct(shape, jnp.float32)
            for shape in (
                (rows, LANES),
                (2, cells_z, 2, 5, rows_y // LANES // 2, LANES),
                (2, 2, rows_y // LANES // 2, LANES),
            )
        ),
        in_specs=[VMEM],
        out_specs=(VMEM,) * 3,
        compiler_params=pltpu.CompilerParams(vmem_limit_bytes=12 << 20),
        cost_estimate=pl.CostEstimate(flops=10**6, bytes_accessed=10**6, transcendentals=0),
        name="widen",
    )(volume)


def put_layers(scratch, rows_y, depth_a, depth_b):
    cells_x = depth_a.shape[0]
    layers = Field(scratch, rows_y, 2 * cells_x)
    odd_depth = parity("depth")
    layers.put((1 - odd_depth) * cells_x, depth_a[...].astype(jnp.float32))
    layers.put(odd_depth * cells_x, depth_b[...].astype(jnp.float32) * inside("depth"))
    return layers


def inner_kernel(cells_z, depth_total, rows, depth_a, depth_b, out, scratch):
    cells_x, rows_y = depth_a.shape
    field = Field(rows, rows_y, cells_x * cells_z)
    layers = put_layers(scratch, rows_y, depth_a, depth_b)

    def columns(i, _):
        for x in (2 * i + 1, 2 * i + 2):
            at = x * cells_z
            sides = (field, at - cells_z), (field, at + cells_z), (layers, x), (layers, cells_x + x)
            store_column(out, x - 1, march(field, cells_z, at, *sides, depth_total))
        return 0

    lax.fori_loop(0, (cells_x - 2) // 2, columns, 0)


def inner(rows, depth_a, depth_b, cells_z, depth_total):
    cells_x, rows_y = depth_a.shape
    return pl.pallas_call(
        lambda *refs: inner_kernel(cells_z, depth_total, *refs),
        out_shape=jax.ShapeDtypeStruct((cells_x - 2, 4, rows_y // LANES, LANES), jnp.float32),
        in_specs=[VMEM] * 3,
        out_specs=VMEM,
        scratch_shapes=[pltpu.VMEM((Field.shape(rows_y, 2 * cells_x)[1], LANES), jnp.float32)],
        compiler_params=pltpu.CompilerParams(vmem_limit_bytes=12 << 20),
        cost_estimate=pl.CostEstimate(flops=10**8, bytes_accessed=10**7, transcendentals=0),
        name="inner",
    )(rows, depth_a, depth_b)


def outer_kernel(
    depth_total, rows, depth_a, depth_b, tile_a, tile_b, done, saved, passed, kept, given, scratch, ends, edge
):
    cells_z, rows_y = tile_a.shape
    cells_x = done.shape[0] + 2
    odd_tile = parity("tile")
    field = Field(rows, rows_y, cells_x * cells_z)
    layers = put_layers(scratch, rows_y, depth_a, depth_b)
    halo = Field(ends, rows_y, 2 * cells_z)
    halo.put((1 - odd_tile) * cells_z, tile_a[...].astype(jnp.float32))
    halo.put(odd_tile * cells_z, tile_b[...].astype(jnp.float32) * inside("tile"))
    for side, left, right in (
        (0, (halo, 0), (field, cells_z)),
        (1, (field, (cells_x - 2) * cells_z), (halo, cells_z)),
    ):
        x = side * (cells_x - 1)
        sides = left, right, (layers, x), (layers, cells_x + x)
        parts = march_shading(field, cells_z, x * cells_z, *sides, saved.at[side], passed.at[side], depth_total)
        store_column(edge, side, parts)
    upper = parity("depth")
    pieces = cells_x // lax.axis_size("depth")
    half = cells_x // 2
    for i in range(half):
        low = i // pieces * 2 * pieces + i % pieces
        for target, bit in ((kept, upper), (given, 1 - upper)):
            x = low + bit * pieces
            if i == 0:
                target[i] = jnp.where(bit == 0, edge[0], done[pieces - 1])
            elif i == half - 1:
                target[i] = jnp.where(bit == 1, edge[1], done[cells_x - pieces - 2])
            else:
                target[i] = done[x - 1]


def outer(rows, depth_a, depth_b, tile_a, tile_b, done, saved, passed, depth_total):
    cells_z, rows_y = tile_a.shape
    cells_x = done.shape[0] + 2
    half = jax.ShapeDtypeStruct((cells_x // 2, 4, rows_y // LANES, LANES), jnp.float32)
    return pl.pallas_call(
        lambda *refs: outer_kernel(depth_total, *refs),
        out_shape=(half, half),
        in_specs=[VMEM] * 8,
        out_specs=(VMEM, VMEM),
        scratch_shapes=[
            pltpu.VMEM((Field.shape(rows_y, 2 * cells_x)[1], LANES), jnp.float32),
            pltpu.VMEM((Field.shape(rows_y, 2 * cells_z)[1], LANES), jnp.float32),
            pltpu.VMEM((2, 4, rows_y // LANES, LANES), jnp.float32),
        ],
        compiler_params=pltpu.CompilerParams(vmem_limit_bytes=12 << 20),
        cost_estimate=pl.CostEstimate(flops=10**7, bytes_accessed=10**6, transcendentals=0),
        name="outer",
    )(rows, depth_a, depth_b, tile_a, tile_b, done, saved, passed)


def over(own, other, in_front):
    front = [jnp.where(in_front, a, b) for a, b in zip(own, other)]
    back = [jnp.where(in_front, b, a) for a, b in zip(own, other)]
    return [a + front[3] * b for a, b in zip(front[:3], back[:3])] + [front[3] * back[3]]


def encode(channels):
    red, green, blue, passing = channels
    return [
        jnp.exp2(POWER * (jnp.log2(x) + CENTRE)).astype(jnp.bfloat16) for x in (red, green, blue, 1.0 - passing)
    ]


def decode(codes):
    red, green, blue, opacity = [jnp.exp2(jnp.log2(y.astype(jnp.float32)) * (1.0 / POWER) - CENTRE) for y in codes]
    return [red, green, blue, 1.0 - opacity]


def received(block):
    channels = [block[channel] for channel in range(4)]
    return decode(channels) if block.dtype == jnp.bfloat16 else channels


def merge_kernel(section, pieces, kept, other, next_kept, next_given):
    position = lax.axis_index("depth")
    in_front = lax.rem(position // 2**section, 2) == 0
    upper = lax.rem(position // 2 ** (section + 1), 2)
    for i in range(kept.shape[0] // 2):
        low = i // pieces * 2 * pieces + i % pieces
        for target, x in ((next_kept, low + upper * pieces), (next_given, low + (1 - upper) * pieces)):
            channels = over(list(kept[x]), received(other[x]), in_front)
            for channel, value in enumerate(encode(channels) if target is next_given else channels):
                target[i, channel] = value


def merge(kept, other, section, pieces):
    shape = (kept.shape[0] // 2, *kept.shape[1:])
    return pl.pallas_call(
        lambda *refs: merge_kernel(section, pieces, *refs),
        out_shape=(jax.ShapeDtypeStruct(shape, jnp.float32), jax.ShapeDtypeStruct(shape, jnp.bfloat16)),
        in_specs=[VMEM] * 2,
        out_specs=(VMEM, VMEM),
        compiler_params=pltpu.CompilerParams(vmem_limit_bytes=8 << 20),
        name="merge",
    )(kept, other)


def finish_kernel(section, kept, other, image):
    position = lax.axis_index("depth")
    in_front = lax.rem(position // 2**section, 2) == 0
    columns, _, chunks, _ = kept.shape
    for x in range(columns):
        red, green, blue, passing = over(list(kept[x]), received(other[x]), in_front)
        for channel, value in enumerate((red, green, blue, 1.0 - passing)):
            for c in range(chunks):
                image[channel, pl.ds(x, 1), pl.ds(c * LANES, LANES)] = value[c : c + 1]


def finish(kept, other, section):
    columns, channels, chunks, _ = kept.shape
    return pl.pallas_call(
        lambda section_kept, section_other, image: finish_kernel(section, section_kept, section_other, image),
        out_shape=jax.ShapeDtypeStruct((channels, columns, chunks * LANES), kept.dtype),
        in_specs=[VMEM] * 2,
        out_specs=VMEM,
        compiler_params=pltpu.CompilerParams(vmem_limit_bytes=8 << 20),
        name="finish",
    )(kept, other)


def shards(volume):
    depth_count = lax.axis_size("depth")
    depth_total = volume.shape[1] * depth_count
    pieces = volume.shape[0] // depth_count
    levels = depth_count.bit_length() - 1
    tile_a, tile_b, depth_a, depth_b = faces(volume)
    tile_b = exchange(tile_b, "tile", 1)
    depth_b = exchange(depth_b, "depth", 1)
    depth_a = exchange(depth_a, "depth", 0)
    tile_a = exchange(tile_a, "tile", 0)
    rows, saved, passed = widen(volume, depth_total)
    done = inner(rows, depth_a, depth_b, volume.shape[1], depth_total)
    kept, given = outer(rows, depth_a, depth_b, tile_a, tile_b, done, saved, passed, depth_total)
    for section in range(levels):
        other = lax.ppermute(given, "depth", [(i, i ^ 1 << section) for i in range(depth_count)])
        if section < levels - 1:
            kept, given = merge(kept, other, section, pieces)
    return finish(kept, other, levels - 1)


def solution(mesh):
    in_specs = (P("tile", "depth", None),)
    out_specs = P(None, ("tile", "depth"), None)
    return jax.shard_map(shards, mesh=mesh, in_specs=in_specs, out_specs=out_specs, check_vma=False)
```
